128 devices in a mesh: ctx: 16 (over y, z), seq: 8 (over x, core).
Axes of the slice: x: 4, y: 4, z: 4, core: 2. Of those that a mesh axis runs over, the one named last changes fastest.
Arguments:
- mixer_input: bfloat16 [16384, 16384], P(('seq', 'ctx')), may hold values from -6 to 6
- step_raw: bfloat16 [16384, 256], P(('seq', 'ctx')), may hold values from -7 to 2.5
- b_proj: bfloat16 [16384, 2048], P(('seq', 'ctx')), may hold values from -3 to 3
- c_proj: bfloat16 [16384, 2048], P(('seq', 'ctx')), may hold values from -0.375 to 0.375
- step_bias: float32 [256], replicated, may hold values from -2 to 2
- decay_log: float32 [256], replicated, may hold values from -3.9 to -2.5
- skip_gain: float32 [256], replicated, may hold values from 0.5 to 1.5
Outputs:
- mixer_output: bfloat16 [16384, 16384], P(('seq', 'ctx'))
The draws below stay inside these ranges and needn't reach their ends.
All inputs are finite; a program needn't handle non-finite values.
Results may differ from the reference program's by a relative error of at most 0.0044.
Values may be sent and summed in bfloat16 or wider, within the bound.
A program may use at most 192 MiB of HBM per device.

```python
import jax
import jax.numpy as jnp
from jax import lax

MIXER_LANES = 256
P_SIZE = 64
N = 256
G = 8
Q = 128
TOK_DEV = 128
CONTEXT_LENGTH = 16384
HP = 16384
GN = 2048


def draw_step_raw(key, part):
    input_matrix_b = jax.random.split(jax.random.fold_in(key, 17), 3)
    drawn_recurrence_check = jax.random.uniform(input_matrix_b[0], (MIXER_LANES,)) < 0.5
    base = jnp.where(drawn_recurrence_check, -5.0, 0.0).astype(jnp.float32)
    shards = CONTEXT_LENGTH // TOK_DEV
    shard_shift = jax.random.uniform(input_matrix_b[1], (shards, 1, MIXER_LANES), jnp.float32, -1.0, 1.0)
    shard_shift = jnp.broadcast_to(shard_shift, (shards, TOK_DEV, MIXER_LANES)).reshape(CONTEXT_LENGTH, MIXER_LANES)
    rough = 0.5 * jax.random.normal(input_matrix_b[2], (CONTEXT_LENGTH, MIXER_LANES), jnp.float32)
    mixer_feature_matrix = base[None, :] + shard_shift + rough
    return jnp.clip(mixer_feature_matrix, -7.0, 2.5).astype(jnp.bfloat16)


def block_scale(own_key, shape, pieces, low, top_value):
    factor_of = 1.0
    for axis_at, shards_of in pieces:
        draws = jax.random.uniform(jax.random.fold_in(jax.random.fold_in(own_key, 6), axis_at), (shards_of,), jnp.float32, low / len(pieces), top_value / len(pieces))
        factor_of = factor_of * jnp.repeat(jnp.exp(draws), shape[axis_at] // shards_of).reshape((-1,) + (1,) * (len(shape) - 1 - axis_at))
    return factor_of


def normal_values(rng, dims, scale, limit, cuts=(), dtype=jnp.bfloat16):
    values = jax.random.normal(rng, dims, jnp.float32) * scale
    if len(cuts) > 0:
        values = block_scale(rng, dims, cuts, -0.22, 0.18) * values
    return jnp.clip(values, min=-limit, max=limit).astype(dtype)


def setup_inputs(seed: int = 0) -> dict:
    streams_of = jax.random.split(jax.random.key(seed), 8)
    mixer_input = normal_values(streams_of[0], (CONTEXT_LENGTH, HP), 1.0, 6.0, ((0, 128),))
    step_raw = draw_step_raw(jax.random.fold_in(streams_of[7], 71), 0)
    b_proj = normal_values(streams_of[2], (CONTEXT_LENGTH, GN), 0.5, 3.0, ((0, 128),))
    c_proj = normal_values(streams_of[3], (CONTEXT_LENGTH, GN), N ** -0.5, 0.375, ((0, 128),))
    step_bias = normal_values(streams_of[4], (MIXER_LANES,), 0.5, 2.0, (), jnp.float32)
    decay_log = jnp.clip(jax.random.uniform(streams_of[5], (MIXER_LANES,), jnp.float32, -3.9, -2.5), -3.9, -2.5)
    skip_gain = jnp.clip(jax.random.uniform(streams_of[6], (MIXER_LANES,), jnp.float32, 0.5, 1.5), 0.5, 1.5)
    return dict(mixer_input=mixer_input, step_raw=step_raw, b_proj=b_proj, c_proj=c_proj, step_bias=step_bias, decay_log=decay_log, skip_gain=skip_gain)


def span_parts(inputs_x, step_size, neg_rate, b_span, c_span, groups):
    count, length, heads = step_size.shape
    share = heads // groups
    cum = jnp.cumsum(step_size * neg_rate, axis=1)
    inner = jnp.einsum("cign,cjgn->cgij", c_span.astype(jnp.float32), b_span.astype(jnp.float32), precision=lax.Precision.HIGHEST)
    cum_t = jnp.transpose(cum, (0, 2, 1))
    diff = cum_t[:, :, :, None] - cum_t[:, :, None, :]
    rows = lax.broadcasted_iota(jnp.int32, (length, length), 0)
    cols = lax.broadcasted_iota(jnp.int32, (length, length), 1)
    decay = jnp.exp(jnp.where(rows >= cols, diff, -jnp.inf))
    step_t = jnp.transpose(step_size, (0, 2, 1))
    scores = inner[:, :, None] * decay.reshape(count, groups, share, length, length) * step_t.reshape(count, groups, share, 1, length)
    scores = scores.reshape(count, heads, length, length).astype(jnp.bfloat16)
    diag = jnp.einsum("chij,cjhp->cihp", scores.astype(jnp.float32), inputs_x.astype(jnp.float32), precision=lax.Precision.HIGHEST)
    tail = jnp.exp(cum[:, -1:, :] - cum) * step_size
    weighted = b_span.astype(jnp.float32)[:, :, :, None, :] * tail.reshape(count, length, groups, share, 1)
    weighted = weighted.reshape(count, length, heads, b_span.shape[3]).astype(jnp.bfloat16)
    states = jnp.einsum("cjhn,cjhp->chnp", weighted.astype(jnp.float32), inputs_x.astype(jnp.float32), precision=lax.Precision.HIGHEST)
    return diag, states, cum


def off_part(c_span, entry_bf, cum, groups):
    count, length, heads = cum.shape
    share = heads // groups
    width = entry_bf.shape[2]
    depth = entry_bf.shape[3]
    outer = jnp.einsum("cign,cgknp->cigkp", c_span.astype(jnp.float32), entry_bf.reshape(count, groups, share, width, depth).astype(jnp.float32), precision=lax.Precision.HIGHEST)
    return outer.reshape(count, length, heads, depth) * jnp.exp(cum)[..., None]


def reference(mixer_input, step_raw, b_proj, c_proj, step_bias, decay_log, skip_gain):
    total = mixer_input.shape[0]
    spans = total // Q
    step_size = jax.nn.softplus(step_raw.astype(jnp.float32) + step_bias)
    neg_rate = -jnp.exp(decay_log)
    inputs_all = mixer_input.reshape(spans, 1, Q, MIXER_LANES, P_SIZE)
    steps_all = step_size.reshape(spans, 1, Q, MIXER_LANES)
    b_all = b_proj.reshape(spans, 1, Q, G, N)
    c_all = c_proj.reshape(spans, 1, Q, G, N)

    def advance(carry, items):
        inputs_x, step_span, b_span, c_span = items
        diag, states, cum = span_parts(inputs_x, step_span, neg_rate, b_span, c_span, G)
        entry_bf = carry.astype(jnp.bfloat16)[None]
        off = off_part(c_span, entry_bf, cum, G)
        result = (diag + off + skip_gain[:, None] * inputs_x.astype(jnp.float32)).astype(jnp.bfloat16)
        carry_next = jnp.exp(cum[0, -1, :])[:, None, None] * carry + states[0]
        return carry_next, result

    start = jnp.zeros((MIXER_LANES, N, P_SIZE), jnp.float32)
    _, outputs = lax.scan(advance, start, (inputs_all, steps_all, b_all, c_all))
    return outputs.reshape(total, MIXER_LANES * P_SIZE)
```

```python
import functools

import jax
import jax.numpy as jnp
from jax import lax
from jax.experimental import pallas as pl
from jax.experimental.pallas import tpu as pltpu
from jax.sharding import PartitionSpec as P

P_SIZE = 64
N = 256
CHUNKS = 4


def scan_kernel(
    nc,
    ns,
    groups,
    x_hbm,
    step_ref,
    b_hbm,
    c_hbm,
    bias_ref,
    dlog_ref,
    gain_ref,
    o_hbm,
    xv,
    bv,
    cv,
    xw,
    spread,
    w2,
    ec2,
    dsend,
    rb,
    rc,
    rx,
    rd,
    states,
    whole,
    cin,
    cout,
    offs,
    offr,
    part,
    load_sem,
    sb_sem,
    sc_sem,
    sd_sem,
    sx_sem,
    so_sem,
    sch_sem,
    rb_sem,
    rc_sem,
    rd_sem,
    rx_sem,
    ro_sem,
    rch_sem,
    out_sem,
):
    f32, bf16 = jnp.float32, jnp.bfloat16
    me = lax.axis_index("ctx")
    sq = lax.axis_index("seq")
    tok, width = xv.shape
    heads = step_ref.shape[1]
    own = width // nc
    cw = own // CHUNKS
    share = heads // groups
    gw = share * P_SIZE
    rep = nc // groups

    loads = (
        pltpu.make_async_copy(x_hbm, xv, load_sem.at[0]),
        pltpu.make_async_copy(b_hbm, bv, load_sem.at[1]),
        pltpu.make_async_copy(c_hbm, cv, load_sem.at[2]),
    )
    for load in loads:
        load.start()

    barrier = pltpu.get_barrier_semaphore()

    def greet(k, carry):
        pl.semaphore_signal(barrier, inc=1, device_id={"ctx": lax.rem(me + k, nc)})
        return carry

    lax.fori_loop(1, nc, greet, 0)

    @pl.when(sq > 0)
    def _():
        pl.semaphore_signal(barrier, inc=1, device_id={"seq": sq - 1})

    @pl.when(sq < ns - 1)
    def _():
        pl.semaphore_signal(barrier, inc=1, device_id={"seq": sq + 1})

    links = (sq > 0).astype(jnp.int32) + (sq < ns - 1).astype(jnp.int32)
    pl.semaphore_wait(barrier, nc - 1 + links)

    def columns(start, size):
        return pl.ds(pl.multiple_of(start, 128), size)

    def send_group(src, dst, send_sem, recv_sem):
        def one(k, carry):
            peer = lax.rem(me + k, nc)
            pltpu.make_async_remote_copy(
                src_ref=src.at[:, columns(lax.div(peer, rep) * N, N)],
                dst_ref=dst.at[me],
                send_sem=send_sem,
                recv_sem=recv_sem,
                device_id={"ctx": peer},
            ).start()
            return carry

        lax.fori_loop(1, nc, one, 0)

    def send_x(c):
        def one(k, carry):
            peer = lax.rem(me + k, nc)
            pltpu.make_async_remote_copy(
                src_ref=xw.at[:, columns(peer * own + c * cw, cw)],
                dst_ref=rx.at[c, me],
                send_sem=sx_sem.at[c],
                recv_sem=rx_sem.at[c],
                device_id={"ctx": peer},
            ).start()
            return carry

        lax.fori_loop(1, nc, one, 0)
        pltpu.make_async_copy(
            xw.at[:, columns(me * own + c * cw, cw)], rx.at[c, me], rx_sem.at[c]
        ).start()

    send_group(b_hbm, rb, sb_sem, rb_sem)

    v = step_ref[...].astype(f32) + bias_ref[...]
    dt = jnp.maximum(v, 0.0) + jnp.log1p(jnp.exp(-jnp.abs(v)))
    rate = dt * (-jnp.exp(dlog_ref[...]))
    rows = lax.broadcasted_iota(jnp.int32, (tok, tok), 0)
    cols = lax.broadcasted_iota(jnp.int32, (tok, tok), 1)
    tri = (rows >= cols).astype(f32)
    cum = jnp.dot(tri, rate, precision=lax.Precision.HIGHEST, preferred_element_type=f32)
    w = dt * jnp.exp(-cum)
    ec = jnp.exp(cum)
    w_hi = w.astype(bf16)
    w_lo = (w - w_hi.astype(f32)).astype(bf16)
    e_hi = ec.astype(bf16)
    e_lo = (ec - e_hi.astype(f32)).astype(bf16)
    gain = jnp.broadcast_to(gain_ref[...], (16, heads))
    g_hi = gain.astype(bf16)
    g_lo = (gain - g_hi.astype(f32)).astype(bf16)
    for g in range(groups):
        part_of = slice(g * share, (g + 1) * share)
        w2[g, :, :share] = w_hi[:, part_of]
        w2[g, :, share:] = w_lo[:, part_of]
        ec2[g, :tok, :share] = e_hi[:, part_of]
        ec2[g, :tok, share:] = e_lo[:, part_of]
        ec2[g, tok:, :share] = g_hi[:, part_of]
        ec2[g, tok:, share:] = g_lo[:, part_of]
    slot_of = lax.broadcasted_iota(jnp.int32, (2 * share, gw), 0)
    lane_of = lax.broadcasted_iota(jnp.int32, (2 * share, gw), 1)
    spread[...] = jnp.where(lax.rem(slot_of, share) == lax.div(lane_of, P_SIZE), 1.0, 0.0).astype(bf16)

    ends = lax.dot_general(
        rate,
        jnp.ones((tok, 128), f32),
        (((0,), (0,)), ((), ())),
        precision=lax.Precision.HIGHEST,
        preferred_element_type=f32,
    )
    head_of = lax.broadcasted_iota(jnp.int32, (heads, 128), 0)
    half_of = lax.div(lax.broadcasted_iota(jnp.int32, (heads, 128), 1), P_SIZE)
    halves = jnp.where(lax.rem(head_of, 2) == half_of, jnp.exp(ends), 0.0)
    pair_row = lax.broadcasted_iota(jnp.int32, (heads // 2, heads), 0)
    pair_col = lax.div(lax.broadcasted_iota(jnp.int32, (heads // 2, heads), 1), 2)
    pick = (pair_row == pair_col).astype(f32)
    tiles = jnp.dot(pick, halves, precision=lax.Precision.HIGHEST, preferred_element_type=f32)
    dsend[...] = tiles.reshape(nc, own // 128, 128)

    loads[0].wait()

    def weigh(g, carry):
        at = columns(g * gw, gw)
        spread_w = jnp.dot(w2[g], spread[...], preferred_element_type=f32)
        xw[:, at] = (xv[:, at].astype(f32) * spread_w).astype(bf16)
        return carry

    lax.fori_loop(0, groups, weigh, 0)

    def send_d(k, carry):
        peer = lax.rem(me + k, nc)
        pltpu.make_async_remote_copy(
            src_ref=dsend.at[peer],
            dst_ref=rd.at[me],
            send_sem=sd_sem,
            recv_sem=rd_sem,
            device_id={"ctx": peer},
        ).start()
        return carry

    lax.fori_loop(1, nc, send_d, 0)
    pltpu.make_async_copy(dsend.at[me], rd.at[me], rd_sem).start()
    send_x(0)
    send_x(1)
    send_group(c_hbm, rc, sc_sem, rc_sem)
    for c in range(2, CHUNKS):
        send_x(c)

    loads[1].wait()
    loads[2].wait()
    mine = columns(lax.div(me, rep) * N, N)
    pltpu.make_async_copy(bv.at[:, mine], rb.at[me], rb_sem).start()
    pltpu.make_async_copy(cv.at[:, mine], rc.at[me], rc_sem).start()

    def local_part(g):
        at = columns(g * gw, gw)
        state_at = columns(g * N, N)
        inner = lax.dot_general(
            cv[:, state_at], bv[:, state_at], (((1,), (1,)), ((), ())), preferred_element_type=f32
        )
        inner = jnp.where(rows >= cols, inner, 0.0).astype(bf16)
        diag = jnp.dot(inner, xw[:, at], preferred_element_type=f32)
        scale = jnp.dot(ec2[g], spread[...], preferred_element_type=f32)
        part[:, at] = scale[:tok] * diag + scale[tok : tok + 1] * xv[:, at].astype(f32)

    def local_range(low, high):
        def one(g, carry):
            local_part(g)
            return carry

        lax.fori_loop(low, high, one, 0)

    def decay_row(c, s):
        per = cw // 128
        tile = rd[s]
        return jnp.concatenate([tile[c * per + r : c * per + r + 1] for r in range(per)], axis=1)

    def gather_states(c):
        pltpu.make_async_copy(rx.at[c], rx.at[c], rx_sem.at[c]).wait()
        slot = c % 2
        cout[c] = jnp.zeros(cout.shape[1:], f32)

        def one(s, total):
            piece = lax.dot_general(
                rb[s], rx[c, s], (((0,), (0,)), ((), ())), preferred_element_type=f32
            )
            factor = decay_row(c, s)
            states[slot, s] = piece
            cout[c] = factor * (cout[c] + piece)
            return total * factor

        whole[c] = lax.fori_loop(0, nc, one, jnp.ones((1, cw), f32))

    def pass_on(c):
        return pltpu.make_async_remote_copy(
            src_ref=cout.at[c],
            dst_ref=cin.at[c],
            send_sem=sch_sem.at[c],
            recv_sem=rch_sem.at[c],
            device_id={"seq": lax.rem(sq + 1, ns)},
        )

    def chain(c):
        @pl.when(sq > 0)
        def _():
            pass_on(c).wait_recv()

        @pl.when(sq == 0)
        def _():
            cin[c] = jnp.zeros(cin.shape[1:], f32)

        @pl.when(sq < ns - 1)
        def _():
            cout[c] = whole[c] * cin[c] + cout[c]
            pass_on(c).start()

    def read_states(c):
        slot = c % 2

        def one(s, carry):
            entry = cin[c]
            offs[c, s] = jnp.dot(rc[s], entry.astype(bf16), preferred_element_type=f32).astype(bf16)
            cin[c] = decay_row(c, s) * (entry + states[slot, s])
            return carry

        lax.fori_loop(0, nc, one, 0)
        at = columns(me * own + c * cw, cw)

        def send(k, carry):
            peer = lax.rem(me + k, nc)
            pltpu.make_async_remote_copy(
                src_ref=offs.at[c, peer],
                dst_ref=offr.at[:, at],
                send_sem=so_sem.at[c],
                recv_sem=ro_sem.at[c],
                device_id={"ctx": peer},
            ).start()
            return carry

        lax.fori_loop(1, nc, send, 0)
        pltpu.make_async_copy(offs.at[c, me], offr.at[:, at], ro_sem.at[c]).start()

    def combine(c):
        pltpu.make_async_copy(rx.at[c], rx.at[c], ro_sem.at[c]).wait()

        def one(o, carry):
            at = columns(o * own + c * cw, cw)
            within = columns(lax.rem(o, rep) * own + c * cw, cw)
            g = lax.div(o, rep)
            scale = jnp.dot(ec2[g, :tok, :], spread[:, within], preferred_element_type=f32)
            offr[:, at] = (part[:, at] + scale * offr[:, at].astype(f32)).astype(bf16)
            pltpu.make_async_copy(offr.at[:, at], o_hbm.at[:, at], out_sem.at[c]).start()
            return carry

        lax.fori_loop(0, nc, one, 0)

    quarter = groups // 4
    pltpu.make_async_copy(rb, rb, rb_sem).wait()
    pltpu.make_async_copy(rd, rd, rd_sem).wait()
    local_range(0, quarter)
    gather_states(0)
    local_range(quarter, 2 * quarter)
    gather_states(1)
    chain(0)
    pltpu.make_async_copy(rc, rc, rc_sem).wait()
    read_states(0)
    local_range(2 * quarter, 3 * quarter)
    gather_states(2)
    chain(1)
    read_states(1)
    local_range(3 * quarter, groups)
    gather_states(3)
    chain(2)
    read_states(2)
    chain(3)
    read_states(3)
    for c in range(CHUNKS):
        combine(c)

    for c in range(CHUNKS):
        pltpu.make_async_copy(rx.at[c, 1:], rx.at[c, 1:], sx_sem.at[c]).wait()
        pltpu.make_async_copy(offs.at[c, 1:], offs.at[c, 1:], so_sem.at[c]).wait()

        @pl.when(sq < ns - 1)
        def _():
            pass_on(c).wait_send()

    pltpu.make_async_copy(rb.at[1:], rb.at[1:], sb_sem).wait()
    pltpu.make_async_copy(rc.at[1:], rc.at[1:], sc_sem).wait()
    pltpu.make_async_copy(rd.at[1:], rd.at[1:], sd_sem).wait()
    for c in range(CHUNKS):
        pltpu.make_async_copy(rx.at[c], rx.at[c], out_sem.at[c]).wait()


def body(mixer_input, step_raw, b_proj, c_proj, step_bias, decay_log, skip_gain):
    nc, ns = lax.axis_size("ctx"), lax.axis_size("seq")
    tok, width = mixer_input.shape
    heads = step_raw.shape[1]
    groups = b_proj.shape[1] // N
    share = heads // groups
    own = width // nc
    cw = own // CHUNKS
    f32, bf16 = jnp.float32, jnp.bfloat16
    any_spec = pl.BlockSpec(memory_space=pl.ANY)
    vmem_spec = pl.BlockSpec(memory_space=pltpu.VMEM)
    dma = pltpu.SemaphoreType.DMA
    return pl.pallas_call(
        functools.partial(scan_kernel, nc, ns, groups),
        out_shape=jax.ShapeDtypeStruct((tok, width), bf16),
        in_specs=[any_spec, vmem_spec, any_spec, any_spec, vmem_spec, vmem_spec, vmem_spec],
        out_specs=any_spec,
        scratch_shapes=[
            pltpu.VMEM((tok, width), bf16),
            pltpu.VMEM((tok, groups * N), bf16),
            pltpu.VMEM((tok, groups * N), bf16),
            pltpu.VMEM((tok, width), bf16),
            pltpu.VMEM((2 * share, share * P_SIZE), bf16),
            pltpu.VMEM((groups, tok, 2 * share), bf16),
            pltpu.VMEM((groups, tok + 16, 2 * share), bf16),
            pltpu.VMEM((nc, own // 128, 128), f32),
            pltpu.VMEM((nc, tok, N), bf16),
            pltpu.VMEM((nc, tok, N), bf16),
            pltpu.VMEM((CHUNKS, nc, tok, cw), bf16),
            pltpu.VMEM((nc, own // 128, 128), f32),
            pltpu.VMEM((2, nc, N, cw), f32),
            pltpu.VMEM((CHUNKS, 1, cw), f32),
            pltpu.VMEM((CHUNKS, N, cw), f32),
            pltpu.VMEM((CHUNKS, N, cw), f32),
            pltpu.VMEM((CHUNKS, nc, tok, cw), bf16),
            pltpu.VMEM((tok, width), bf16),
            pltpu.VMEM((tok, width), f32),
            dma((3,)),
            dma,
            dma,
            dma,
            dma((CHUNKS,)),
            dma((CHUNKS,)),
            dma((CHUNKS,)),
            dma,
            dma,
            dma,
            dma((CHUNKS,)),
            dma((CHUNKS,)),
            dma((CHUNKS,)),
            dma((CHUNKS,)),
        ],
        compiler_params=pltpu.CompilerParams(
            collective_id=0, has_side_effects=True, vmem_limit_bytes=62 * 1024 * 1024
        ),
    )(
        mixer_input,
        step_raw,
        b_proj,
        c_proj,
        step_bias.reshape(1, heads),
        decay_log.reshape(1, heads),
        skip_gain.reshape(1, heads),
    )


def solution(mesh):
    return jax.shard_map(
        body,
        mesh=mesh,
        in_specs=(
            P(("seq", "ctx"), None),
            P(("seq", "ctx"), None),
            P(("seq", "ctx"), None),
            P(("seq", "ctx"), None),
            P(),
            P(),
            P(),
        ),
        out_specs=P(("seq", "ctx"), None),
        check_vma=False,
    )
```

```python
import functools

import jax
import jax.numpy as jnp
from jax import lax
from jax.experimental import pallas as pl
from jax.experimental.pallas import tpu as pltpu
from jax.sharding import PartitionSpec as P

P_SIZE = 64
N = 256
CHUNKS = 4


def scan_kernel(
    nc,
    ns,
    groups,
    x_hbm,
    step_ref,
    b_hbm,
    c_hbm,
    bias_ref,
    dlog_ref,
    gain_ref,
    o_hbm,
    xv,
    bv,
    cv,
    xw,
    spread,
    w2,
    ec2,
    dsend,
    rb,
    rc,
    rx,
    rd,
    states,
    whole,
    cin,
    cout,
    offs,
    offr,
    part,
    load_sem,
    sb_sem,
    sc_sem,
    sd_sem,
    sx_sem,
    so_sem,
    sch_sem,
    rb_sem,
    rc_sem,
    rd_sem,
    rx_sem,
    ro_sem,
    rch_sem,
    out_sem,
):
    f32, bf16 = jnp.float32, jnp.bfloat16
    me = lax.axis_index("ctx")
    sq = lax.axis_index("seq")
    tok, width = xv.shape
    heads = step_ref.shape[1]
    own = width // nc
    cw = own // CHUNKS
    share = heads // groups
    gw = share * P_SIZE
    rep = nc // groups

    side = 4 if nc % 4 == 0 else 1
    rank = nc // side
    row, col = lax.div(me, side), lax.rem(me, side)

    def partner(k):
        return lax.rem(row + lax.div(k, side), rank) * side + lax.rem(col + lax.rem(k, side), side)

    loads = (
        pltpu.make_async_copy(x_hbm, xv, load_sem.at[0]),
        pltpu.make_async_copy(b_hbm, bv, load_sem.at[1]),
        pltpu.make_async_copy(c_hbm, cv, load_sem.at[2]),
    )
    for load in loads:
        load.start()

    barrier = pltpu.get_barrier_semaphore()

    def greet(k, carry):
        pl.semaphore_signal(barrier, inc=1, device_id={"ctx": partner(k)})
        return carry

    lax.fori_loop(1, nc, greet, 0)

    @pl.when(sq > 0)
    def _():
        pl.semaphore_signal(barrier, inc=1, device_id={"seq": sq - 1})

    @pl.when(sq < ns - 1)
    def _():
        pl.semaphore_signal(barrier, inc=1, device_id={"seq": sq + 1})

    links = (sq > 0).astype(jnp.int32) + (sq < ns - 1).astype(jnp.int32)
    pl.semaphore_wait(barrier, nc - 1 + links)

    def columns(start, size):
        return pl.ds(pl.multiple_of(start, 128), size)

    def send_group(src, dst, send_sem, recv_sem):
        def one(k, carry):
            peer = partner(k)
            pltpu.make_async_remote_copy(
                src_ref=src.at[:, columns(lax.div(peer, rep) * N, N)],
                dst_ref=dst.at[me],
                send_sem=send_sem,
                recv_sem=recv_sem,
                device_id={"ctx": peer},
            ).start()
            return carry

        lax.fori_loop(1, nc, one, 0)

    def send_x(c):
        def one(k, carry):
            peer = partner(k)
            pltpu.make_async_remote_copy(
                src_ref=xw.at[:, columns(peer * own + c * cw, cw)],
                dst_ref=rx.at[c, me],
                send_sem=sx_sem.at[c],
                recv_sem=rx_sem.at[c],
                device_id={"ctx": peer},
            ).start()
            return carry

        lax.fori_loop(1, nc, one, 0)
        pltpu.make_async_copy(
            xw.at[:, columns(me * own + c * cw, cw)], rx.at[c, me], rx_sem.at[c]
        ).start()

    send_group(b_hbm, rb, sb_sem, rb_sem)

    v = step_ref[...].astype(f32) + bias_ref[...]
    dt = jnp.maximum(v, 0.0) + jnp.log1p(jnp.exp(-jnp.abs(v)))
    rate = dt * (-jnp.exp(dlog_ref[...]))
    rows = lax.broadcasted_iota(jnp.int32, (tok, tok), 0)
    cols = lax.broadcasted_iota(jnp.int32, (tok, tok), 1)
    tri = (rows >= cols).astype(f32)
    cum = jnp.dot(tri, rate, precision=lax.Precision.HIGHEST, preferred_element_type=f32)
    w = dt * jnp.exp(-cum)
    ec = jnp.exp(cum)
    w_hi = w.astype(bf16)
    w_lo = (w - w_hi.astype(f32)).astype(bf16)
    e_hi = ec.astype(bf16)
    e_lo = (ec - e_hi.astype(f32)).astype(bf16)
    gain = jnp.broadcast_to(gain_ref[...], (16, heads))
    g_hi = gain.astype(bf16)
    g_lo = (gain - g_hi.astype(f32)).astype(bf16)
    for g in range(groups):
        part_of = slice(g * share, (g + 1) * share)
        w2[g, :, :share] = w_hi[:, part_of]
        w2[g, :, share:] = w_lo[:, part_of]
        ec2[g, :tok, :share] = e_hi[:, part_of]
        ec2[g, :tok, share:] = e_lo[:, part_of]
        ec2[g, tok:, :share] = g_hi[:, part_of]
        ec2[g, tok:, share:] = g_lo[:, part_of]
    slot_of = lax.broadcasted_iota(jnp.int32, (2 * share, gw), 0)
    lane_of = lax.broadcasted_iota(jnp.int32, (2 * share, gw), 1)
    spread[...] = jnp.where(lax.rem(slot_of, share) == lax.div(lane_of, P_SIZE), 1.0, 0.0).astype(bf16)

    ends = lax.dot_general(
        rate,
        jnp.ones((tok, 128), f32),
        (((0,), (0,)), ((), ())),
        precision=lax.Precision.HIGHEST,
        preferred_element_type=f32,
    )
    head_of = lax.broadcasted_iota(jnp.int32, (heads, 128), 0)
    half_of = lax.div(lax.broadcasted_iota(jnp.int32, (heads, 128), 1), P_SIZE)
    halves = jnp.where(lax.rem(head_of, 2) == half_of, jnp.exp(ends), 0.0)
    pair_row = lax.broadcasted_iota(jnp.int32, (heads // 2, heads), 0)
    pair_col = lax.div(lax.broadcasted_iota(jnp.int32, (heads // 2, heads), 1), 2)
    pick = (pair_row == pair_col).astype(f32)
    tiles = jnp.dot(pick, halves, precision=lax.Precision.HIGHEST, preferred_element_type=f32)
    dsend[...] = tiles.reshape(nc, own // 128, 128)

    loads[0].wait()

    def weigh(g, carry):
        at = columns(g * gw, gw)
        spread_w = jnp.dot(w2[g], spread[...], preferred_element_type=f32)
        xw[:, at] = (xv[:, at].astype(f32) * spread_w).astype(bf16)
        return carry

    lax.fori_loop(0, groups, weigh, 0)

    def send_d(k, carry):
        peer = partner(k)
        pltpu.make_async_remote_copy(
            src_ref=dsend.at[peer],
            dst_ref=rd.at[me],
            send_sem=sd_sem,
            recv_sem=rd_sem,
            device_id={"ctx": peer},
        ).start()
        return carry

    lax.fori_loop(1, nc, send_d, 0)
    pltpu.make_async_copy(dsend.at[me], rd.at[me], rd_sem).start()
    send_x(0)
    send_x(1)
    send_group(c_hbm, rc, sc_sem, rc_sem)
    for c in range(2, CHUNKS):
        send_x(c)

    loads[1].wait()
    loads[2].wait()
    mine = columns(lax.div(me, rep) * N, N)
    pltpu.make_async_copy(bv.at[:, mine], rb.at[me], rb_sem).start()
    pltpu.make_async_copy(cv.at[:, mine], rc.at[me], rc_sem).start()

    def local_part(g):
        at = columns(g * gw, gw)
        state_at = columns(g * N, N)
        inner = lax.dot_general(
            cv[:, state_at], bv[:, state_at], (((1,), (1,)), ((), ())), preferred_element_type=f32
        )
        inner = jnp.where(rows >= cols, inner, 0.0).astype(bf16)
        diag = jnp.dot(inner, xw[:, at], preferred_element_type=f32)
        scale = jnp.dot(ec2[g], spread[...], preferred_element_type=f32)
        part[:, at] = scale[:tok] * diag + scale[tok : tok + 1] * xv[:, at].astype(f32)

    def local_range(low, high):
        def one(g, carry):
            local_part(g)
            return carry

        lax.fori_loop(low, high, one, 0)

    def decay_row(c, s):
        per = cw // 128
        tile = rd[s]
        return jnp.concatenate([tile[c * per + r : c * per + r + 1] for r in range(per)], axis=1)

    def gather_states(c):
        pltpu.make_async_copy(rx.at[c], rx.at[c], rx_sem.at[c]).wait()
        slot = c % 2
        cout[c] = jnp.zeros(cout.shape[1:], f32)

        def one(s, total):
            piece = lax.dot_general(
                rb[s], rx[c, s], (((0,), (0,)), ((), ())), preferred_element_type=f32
            )
            factor = decay_row(c, s)
            states[slot, s] = piece
            cout[c] = factor * (cout[c] + piece)
            return total * factor

        whole[c] = lax.fori_loop(0, nc, one, jnp.ones((1, cw), f32))

    def pass_on(c):
        return pltpu.make_async_remote_copy(
            src_ref=cout.at[c],
            dst_ref=cin.at[c],
            send_sem=sch_sem.at[c],
            recv_sem=rch_sem.at[c],
            device_id={"seq": lax.rem(sq + 1, ns)},
        )

    def chain(c):
        @pl.when(sq > 0)
        def _():
            pass_on(c).wait_recv()

        @pl.when(sq == 0)
        def _():
            cin[c] = jnp.zeros(cin.shape[1:], f32)

        @pl.when(sq < ns - 1)
        def _():
            cout[c] = whole[c] * cin[c] + cout[c]
            pass_on(c).start()

    def read_states(c):
        slot = c % 2

        def one(s, carry):
            entry = cin[c]
            offs[c, s] = jnp.dot(rc[s], entry.astype(bf16), preferred_element_type=f32).astype(bf16)
            cin[c] = decay_row(c, s) * (entry + states[slot, s])
            return carry

        lax.fori_loop(0, nc, one, 0)
        at = columns(me * own + c * cw, cw)

        def send(k, carry):
            peer = partner(k)
            pltpu.make_async_remote_copy(
                src_ref=offs.at[c, peer],
                dst_ref=offr.at[:, at],
                send_sem=so_sem.at[c],
                recv_sem=ro_sem.at[c],
                device_id={"ctx": peer},
            ).start()
            return carry

        lax.fori_loop(1, nc, send, 0)
        pltpu.make_async_copy(offs.at[c, me], offr.at[:, at], ro_sem.at[c]).start()

    def combine(c):
        pltpu.make_async_copy(rx.at[c], rx.at[c], ro_sem.at[c]).wait()

        def one(o, carry):
            at = columns(o * own + c * cw, cw)
            within = columns(lax.rem(o, rep) * own + c * cw, cw)
            g = lax.div(o, rep)
            scale = jnp.dot(ec2[g, :tok, :], spread[:, within], preferred_element_type=f32)
            offr[:, at] = (part[:, at] + scale * offr[:, at].astype(f32)).astype(bf16)
            pltpu.make_async_copy(offr.at[:, at], o_hbm.at[:, at], out_sem.at[c]).start()
            return carry

        lax.fori_loop(0, nc, one, 0)

    quarter = groups // 4
    pltpu.make_async_copy(rb, rb, rb_sem).wait()
    pltpu.make_async_copy(rd, rd, rd_sem).wait()
    local_range(0, quarter)
    gather_states(0)
    local_range(quarter, 2 * quarter)
    gather_states(1)
    chain(0)
    pltpu.make_async_copy(rc, rc, rc_sem).wait()
    read_states(0)
    local_range(2 * quarter, 3 * quarter)
    gather_states(2)
    chain(1)
    read_states(1)
    local_range(3 * quarter, groups)
    gather_states(3)
    chain(2)
    read_states(2)
    chain(3)
    read_states(3)
    for c in range(CHUNKS):
        combine(c)

    for c in range(CHUNKS):
        pltpu.make_async_copy(rx.at[c, 1:], rx.at[c, 1:], sx_sem.at[c]).wait()
        pltpu.make_async_copy(offs.at[c, 1:], offs.at[c, 1:], so_sem.at[c]).wait()

        @pl.when(sq < ns - 1)
        def _():
            pass_on(c).wait_send()

    pltpu.make_async_copy(rb.at[1:], rb.at[1:], sb_sem).wait()
    pltpu.make_async_copy(rc.at[1:], rc.at[1:], sc_sem).wait()
    pltpu.make_async_copy(rd.at[1:], rd.at[1:], sd_sem).wait()
    for c in range(CHUNKS):
        pltpu.make_async_copy(rx.at[c], rx.at[c], out_sem.at[c]).wait()


def body(mixer_input, step_raw, b_proj, c_proj, step_bias, decay_log, skip_gain):
    nc, ns = lax.axis_size("ctx"), lax.axis_size("seq")
    tok, width = mixer_input.shape
    heads = step_raw.shape[1]
    groups = b_proj.shape[1] // N
    share = heads // groups
    own = width // nc
    cw = own // CHUNKS
    f32, bf16 = jnp.float32, jnp.bfloat16
    any_spec = pl.BlockSpec(memory_space=pl.ANY)
    vmem_spec = pl.BlockSpec(memory_space=pltpu.VMEM)
    dma = pltpu.SemaphoreType.DMA
    return pl.pallas_call(
        functools.partial(scan_kernel, nc, ns, groups),
        out_shape=jax.ShapeDtypeStruct((tok, width), bf16),
        in_specs=[any_spec, vmem_spec, any_spec, any_spec, vmem_spec, vmem_spec, vmem_spec],
        out_specs=any_spec,
        scratch_shapes=[
            pltpu.VMEM((tok, width), bf16),
            pltpu.VMEM((tok, groups * N), bf16),
            pltpu.VMEM((tok, groups * N), bf16),
            pltpu.VMEM((tok, width), bf16),
            pltpu.VMEM((2 * share, share * P_SIZE), bf16),
            pltpu.VMEM((groups, tok, 2 * share), bf16),
            pltpu.VMEM((groups, tok + 16, 2 * share), bf16),
            pltpu.VMEM((nc, own // 128, 128), f32),
            pltpu.VMEM((nc, tok, N), bf16),
            pltpu.VMEM((nc, tok, N), bf16),
            pltpu.VMEM((CHUNKS, nc, tok, cw), bf16),
            pltpu.VMEM((nc, own // 128, 128), f32),
            pltpu.VMEM((2, nc, N, cw), f32),
            pltpu.VMEM((CHUNKS, 1, cw), f32),
            pltpu.VMEM((CHUNKS, N, cw), f32),
            pltpu.VMEM((CHUNKS, N, cw), f32),
            pltpu.VMEM((CHUNKS, nc, tok, cw), bf16),
            pltpu.VMEM((tok, width), bf16),
            pltpu.VMEM((tok, width), f32),
            dma((3,)),
            dma,
            dma,
            dma,
            dma((CHUNKS,)),
            dma((CHUNKS,)),
            dma((CHUNKS,)),
            dma,
            dma,
            dma,
            dma((CHUNKS,)),
            dma((CHUNKS,)),
            dma((CHUNKS,)),
            dma((CHUNKS,)),
        ],
        compiler_params=pltpu.CompilerParams(
            collective_id=0, has_side_effects=True, vmem_limit_bytes=62 * 1024 * 1024
        ),
    )(
        mixer_input,
        step_raw,
        b_proj,
        c_proj,
        step_bias.reshape(1, heads),
        decay_log.reshape(1, heads),
        skip_gain.reshape(1, heads),
    )


def solution(mesh):
    return jax.shard_map(
        body,
        mesh=mesh,
        in_specs=(
            P(("seq", "ctx"), None),
            P(("seq", "ctx"), None),
            P(("seq", "ctx"), None),
            P(("seq", "ctx"), None),
            P(),
            P(),
            P(),
        ),
        out_specs=P(("seq", "ctx"), None),
        check_vma=False,
    )
```

```python
import functools

import jax
import jax.numpy as jnp
from jax import lax
from jax.experimental import pallas as pl
from jax.experimental.pallas import tpu as pltpu
from jax.sharding import PartitionSpec as P

P_SIZE = 64
N = 256
CHUNKS = 8
SLOTS = 4


def scan_kernel(
    nc,
    ns,
    groups,
    x_hbm,
    step_ref,
    b_hbm,
    c_hbm,
    bias_ref,
    dlog_ref,
    gain_ref,
    o_ref,
    xv,
    bv,
    cv,
    xw,
    spread,
    w2,
    ec2,
    dsend,
    rb,
    rc,
    rx,
    rd,
    states,
    total,
    whole,
    entry,
    pre,
    pre_d,
    run,
    run_d,
    head,
    nexthead,
    offs,
    offr,
    part,
    load_sem,
    sb_sem,
    sc_sem,
    sd_sem,
    sx_sem,
    so_sem,
    sr_sem,
    srd_sem,
    sh_sem,
    rb_sem,
    rc_sem,
    rd_sem,
    rx_sem,
    ro_sem,
    rr_sem,
    rrd_sem,
    rh_sem,
):
    f32, bf16 = jnp.float32, jnp.bfloat16
    me = lax.axis_index("ctx")
    sq = lax.axis_index("seq")
    tok, width = xv.shape
    heads = step_ref.shape[1]
    cw = width // groups // CHUNKS
    share = heads // groups
    gw = share * P_SIZE
    side = groups // 2
    half, span = lax.div(me, groups), lax.rem(me, groups)
    row, col = lax.div(span, side), lax.rem(span, side)
    flip = half * side
    mine = lax.rem(span + flip, groups)
    across = (1 - half) * groups + lax.rem(span + side, groups)
    role = lax.rem(sq, 2) * 2 + half
    block = lax.div(sq, 2)
    blocks = ns // 2
    inner_x = block < blocks - 1

    def partner(k):
        return lax.rem(row + lax.div(k, side), 2) * side + lax.rem(col + lax.rem(k, side), side)

    def source(k):
        return lax.rem(row + lax.div(k, side), 2) * side + lax.rem(
            col + side - lax.rem(k, side), side
        )

    def group_of(s):
        return lax.rem(s + flip, groups)

    def to_ctx(s):
        return {"ctx": half * groups + s}

    def following():
        return {"ctx": across, "seq": jnp.where(role == 1, sq + 1, sq)}

    def preceding():
        return {"ctx": across, "seq": jnp.where(role == 2, sq - 1, sq)}

    def carrier():
        return {
            "ctx": jnp.where(half == 1, me, across),
            "seq": 2 * block - 1,
        }

    def receiver(r):
        return {"ctx": me if r % 2 == 1 else across, "seq": 2 * block + 2 + r // 2}

    loads = (
        pltpu.make_async_copy(x_hbm, xv, load_sem.at[0]),
        pltpu.make_async_copy(b_hbm, bv, load_sem.at[1]),
        pltpu.make_async_copy(c_hbm, cv, load_sem.at[2]),
    )
    for load in loads:
        load.start()

    barrier = pltpu.get_barrier_semaphore()

    def greet(k, carry):
        pl.semaphore_signal(barrier, inc=1, device_id=to_ctx(partner(k)))
        return carry

    lax.fori_loop(1, groups, greet, 0)

    @pl.when(role > 0)
    def _():
        pl.semaphore_signal(barrier, inc=1, device_id=preceding())

    @pl.when(role < 3)
    def _():
        pl.semaphore_signal(barrier, inc=1, device_id=following())

    @pl.when(block > 0)
    def _():
        pl.semaphore_signal(barrier, inc=1, device_id=carrier())

    @pl.when((role == 3) & inner_x)
    def _():
        for r in range(4):
            pl.semaphore_signal(barrier, inc=1, device_id=receiver(r))

    friends = (
        groups
        - 1
        + jnp.where(role > 0, 1, 0)
        + jnp.where(role < 3, 1, 0)
        + jnp.where(block > 0, 1, 0)
        + jnp.where((role == 3) & inner_x, 4, 0)
    )
    pl.semaphore_wait(barrier, friends)

    def columns(start, size):
        return pl.ds(pl.multiple_of(start, 128), size)

    def send_group(src, dst, send_sem, recv_sem):
        def one(k, carry):
            peer = partner(k)
            pltpu.make_async_remote_copy(
                src_ref=src.at[:, columns(group_of(peer) * N, N)],
                dst_ref=dst.at[span],
                send_sem=send_sem,
                recv_sem=recv_sem,
                device_id=to_ctx(peer),
            ).start()
            return carry

        lax.fori_loop(1, groups, one, 0)

    def send_x(c):
        def one(k, carry):
            peer = partner(k)
            pltpu.make_async_remote_copy(
                src_ref=xw.at[:, columns(group_of(peer) * gw + c * cw, cw)],
                dst_ref=rx.at[c, span],
                send_sem=sx_sem.at[c],
                recv_sem=rx_sem.at[c],
                device_id=to_ctx(peer),
            ).start()
            return carry

        lax.fori_loop(1, groups, one, 0)
        pltpu.make_async_copy(
            xw.at[:, columns(mine * gw + c * cw, cw)], rx.at[c, span], rx_sem.at[c]
        ).start()

    send_group(b_hbm, rb, sb_sem, rb_sem)

    v = step_ref[...].astype(f32) + bias_ref[...]
    dt = jnp.maximum(v, 0.0) + jnp.log1p(jnp.exp(-jnp.abs(v)))
    rate = dt * (-jnp.exp(dlog_ref[...]))
    rows = lax.broadcasted_iota(jnp.int32, (tok, tok), 0)
    cols = lax.broadcasted_iota(jnp.int32, (tok, tok), 1)
    tri = (rows >= cols).astype(f32)
    cum = jnp.dot(tri, rate, precision=lax.Precision.HIGHEST, preferred_element_type=f32)
    w = dt * jnp.exp(-cum)
    ec = jnp.exp(cum)
    w_hi = w.astype(bf16)
    w_lo = (w - w_hi.astype(f32)).astype(bf16)
    e_hi = ec.astype(bf16)
    e_lo = (ec - e_hi.astype(f32)).astype(bf16)
    gain = jnp.broadcast_to(gain_ref[...], (16, heads))
    g_hi = gain.astype(bf16)
    g_lo = (gain - g_hi.astype(f32)).astype(bf16)
    for g in range(groups):
        part_of = slice(g * share, (g + 1) * share)
        w2[g, :, :share] = w_hi[:, part_of]
        w2[g, :, share:] = w_lo[:, part_of]
        ec2[g, :tok, :share] = e_hi[:, part_of]
        ec2[g, :tok, share:] = e_lo[:, part_of]
        ec2[g, tok:, :share] = g_hi[:, part_of]
        ec2[g, tok:, share:] = g_lo[:, part_of]
    slot_of = lax.broadcasted_iota(jnp.int32, (2 * share, gw), 0)
    lane_of = lax.broadcasted_iota(jnp.int32, (2 * share, gw), 1)
    spread[...] = jnp.where(lax.rem(slot_of, share) == lax.div(lane_of, P_SIZE), 1.0, 0.0).astype(bf16)

    loads[0].wait()

    def weigh(c):
        def one(g, carry):
            at = columns(g * gw + c * cw, cw)
            weight = jnp.dot(w2[g], spread[:, c * cw : (c + 1) * cw], preferred_element_type=f32)
            xw[:, at] = (xv[:, at].astype(f32) * weight).astype(bf16)
            return carry

        lax.fori_loop(0, groups, one, 0)

    weigh(0)
    send_x(0)

    ends = lax.dot_general(
        rate,
        jnp.ones((tok, 128), f32),
        (((0,), (0,)), ((), ())),
        precision=lax.Precision.HIGHEST,
        preferred_element_type=f32,
    )
    head_of = lax.broadcasted_iota(jnp.int32, (heads, 128), 0)
    half_of = lax.div(lax.broadcasted_iota(jnp.int32, (heads, 128), 1), P_SIZE)
    halves = jnp.where(lax.rem(head_of, 2) == half_of, jnp.exp(ends), 0.0)
    pair_row = lax.broadcasted_iota(jnp.int32, (heads // 2, heads), 0)
    pair_col = lax.div(lax.broadcasted_iota(jnp.int32, (heads // 2, heads), 1), 2)
    pick = (pair_row == pair_col).astype(f32)
    tiles = jnp.dot(pick, halves, precision=lax.Precision.HIGHEST, preferred_element_type=f32)
    dsend[...] = tiles.reshape(groups, gw // 128, 128)

    def send_d(k, carry):
        peer = partner(k)
        pltpu.make_async_remote_copy(
            src_ref=dsend.at[group_of(peer)],
            dst_ref=rd.at[span],
            send_sem=sd_sem,
            recv_sem=rd_sem,
            device_id=to_ctx(peer),
        ).start()
        return carry

    lax.fori_loop(1, groups, send_d, 0)
    pltpu.make_async_copy(dsend.at[mine], rd.at[span], rd_sem).start()
    for c in range(1, CHUNKS):
        weigh(c)
        send_x(c)
        if c == 2:
            send_group(c_hbm, rc, sc_sem, rc_sem)

    loads[1].wait()
    loads[2].wait()
    own = columns(mine * N, N)
    pltpu.make_async_copy(bv.at[:, own], rb.at[span], rb_sem).start()
    pltpu.make_async_copy(cv.at[:, own], rc.at[span], rc_sem).start()

    @pl.when(role == 0)
    def _():
        pre[...] = jnp.zeros(pre.shape, bf16)
        pre_d[...] = jnp.ones(pre_d.shape, f32)

    @pl.when(block == 0)
    def _():
        head[...] = jnp.zeros(head.shape, bf16)

    def local_part(g):
        at = slice(g * gw, (g + 1) * gw)
        state_at = slice(g * N, (g + 1) * N)
        inner = lax.dot_general(
            cv[:, state_at], bv[:, state_at], (((1,), (1,)), ((), ())), preferred_element_type=f32
        )
        inner = jnp.where(rows >= cols, inner, 0.0).astype(bf16)

        def one(c, carry):
            at = columns(g * gw + c * cw, cw)
            diag = jnp.dot(inner, xw[:, at], preferred_element_type=f32)
            scale = jnp.dot(ec2[g], spread[:, columns(c * cw, cw)], preferred_element_type=f32)
            part[:, at] = scale[:tok] * diag + scale[tok : tok + 1] * xv[:, at].astype(f32)
            return carry

        lax.fori_loop(0, CHUNKS, one, 0)

    def decay_row(c, s):
        per = cw // 128
        tile = rd[s]
        return jnp.concatenate([tile[c * per + r : c * per + r + 1] for r in range(per)], axis=1)

    def gather_states(c):
        pltpu.make_async_copy(rx.at[c], rx.at[c], rx_sem.at[c]).wait()
        slot = c % SLOTS
        total[c] = jnp.zeros(total.shape[1:], f32)

        def one(s, product):
            piece = lax.dot_general(
                rb[s], rx[c, s], (((0,), (0,)), ((), ())), preferred_element_type=f32
            )
            factor = decay_row(c, s)
            states[slot, s] = piece
            total[c] = factor * (total[c] + piece)
            return product * factor

        whole[c] = lax.fori_loop(0, groups, one, jnp.ones((1, cw), f32))

    def pass_run(c):
        return (
            pltpu.make_async_remote_copy(
                src_ref=run.at[c],
                dst_ref=pre.at[c],
                send_sem=sr_sem.at[c],
                recv_sem=rr_sem.at[c],
                device_id=following(),
            ),
            pltpu.make_async_remote_copy(
                src_ref=run_d.at[c],
                dst_ref=pre_d.at[c],
                send_sem=srd_sem.at[c],
                recv_sem=rrd_sem.at[c],
                device_id=following(),
            ),
        )

    def pass_head(c, r):
        return pltpu.make_async_remote_copy(
            src_ref=nexthead.at[c],
            dst_ref=head.at[c],
            send_sem=sh_sem.at[c, r],
            recv_sem=rh_sem.at[c],
            device_id=receiver(r),
        )

    def compose(c):
        @pl.when(role > 0)
        def _():
            for copy in pass_run(c):
                copy.wait_recv()

        ahead = whole[c] * pre[c].astype(f32) + total[c]
        span_d = whole[c] * pre_d[c, :1]

        @pl.when(role < 3)
        def _():
            run[c] = ahead.astype(bf16)
            run_d[c] = jnp.broadcast_to(span_d, run_d.shape[1:])
            for copy in pass_run(c):
                copy.start()

        @pl.when((role == 3) & inner_x)
        def _():
            total[c] = ahead
            whole[c] = span_d

    def forward(c):
        @pl.when((role == 3) & inner_x)
        def _():
            @pl.when(block > 0)
            def _():
                pass_head(c, 0).wait_recv()

            nexthead[c] = (whole[c] * head[c].astype(f32) + total[c]).astype(bf16)
            for r in (3, 2, 1, 0):
                pass_head(c, r).start()

    def read_states(c):
        @pl.when((block > 0) & ((role < 3) | (block == blocks - 1)))
        def _():
            pass_head(c, 0).wait_recv()

        slot = c % SLOTS
        entry[...] = pre_d[c, :1] * head[c].astype(f32) + pre[c].astype(f32)

        def one(s, carry):
            state = entry[...]
            offs[c, s] = jnp.dot(rc[s], state.astype(bf16), preferred_element_type=f32).astype(bf16)
            entry[...] = decay_row(c, s) * (state + states[slot, s])
            return carry

        lax.fori_loop(0, groups, one, 0)
        at = columns(mine * gw + c * cw, cw)

        def send(k, carry):
            peer = partner(k)
            pltpu.make_async_remote_copy(
                src_ref=offs.at[c, peer],
                dst_ref=offr.at[:, at],
                send_sem=so_sem.at[c],
                recv_sem=ro_sem.at[c, span],
                device_id=to_ctx(peer),
            ).start()
            return carry

        lax.fori_loop(1, groups, send, 0)
        pltpu.make_async_copy(offs.at[c, span], offr.at[:, at], ro_sem.at[c, span]).start()

    def combine(c):
        def one(k, carry):
            s = source(k)
            g = group_of(s)
            at = columns(g * gw + c * cw, cw)
            pltpu.make_async_copy(offs.at[c, 0], offr.at[:, at], ro_sem.at[c, s]).wait()
            scale = jnp.dot(
                ec2[g, :tok, :], spread[:, c * cw : (c + 1) * cw], preferred_element_type=f32
            )
            o_ref[:, at] = (part[:, at] + scale * offr[:, at].astype(f32)).astype(bf16)
            return carry

        lax.fori_loop(0, groups, one, 0)

    pltpu.make_async_copy(rb, rb, rb_sem).wait()
    pltpu.make_async_copy(rd, rd, rd_sem).wait()
    lag = SLOTS - 1
    for c in range(CHUNKS + lag):
        if c < CHUNKS:
            gather_states(c)
            compose(c)
            forward(c)
        if c == lag:
            pltpu.make_async_copy(rc, rc, rc_sem).wait()
        if c >= lag:
            read_states(c - lag)
        if c < groups:
            local_part(c)
    for c in range(CHUNKS):
        combine(c)

    for c in range(CHUNKS):
        pltpu.make_async_copy(rx.at[c, 1:], rx.at[c, 1:], sx_sem.at[c]).wait()
        pltpu.make_async_copy(offs.at[c, 1:], offs.at[c, 1:], so_sem.at[c]).wait()

        @pl.when(role < 3)
        def _():
            for copy in pass_run(c):
                copy.wait_send()

        @pl.when((role == 3) & inner_x)
        def _():
            for r in range(4):
                pass_head(c, r).wait_send()

    pltpu.make_async_copy(rb.at[1:], rb.at[1:], sb_sem).wait()
    pltpu.make_async_copy(rc.at[1:], rc.at[1:], sc_sem).wait()
    pltpu.make_async_copy(rd.at[1:], rd.at[1:], sd_sem).wait()


def body(mixer_input, step_raw, b_proj, c_proj, step_bias, decay_log, skip_gain):
    nc, ns = lax.axis_size("ctx"), lax.axis_size("seq")
    tok, width = mixer_input.shape
    heads = step_raw.shape[1]
    groups = b_proj.shape[1] // N
    share = heads // groups
    gw = share * P_SIZE
    cw = gw // CHUNKS
    f32, bf16 = jnp.float32, jnp.bfloat16
    any_spec = pl.BlockSpec(memory_space=pl.ANY)
    vmem_spec = pl.BlockSpec(memory_space=pltpu.VMEM)
    dma = pltpu.SemaphoreType.DMA
    return pl.pallas_call(
        functools.partial(scan_kernel, nc, ns, groups),
        out_shape=pltpu.VMEM((tok, width), bf16),
        in_specs=[any_spec, vmem_spec, any_spec, any_spec, vmem_spec, vmem_spec, vmem_spec],
        out_specs=vmem_spec,
        scratch_shapes=[
            pltpu.VMEM((tok, width), bf16),
            pltpu.VMEM((tok, groups * N), bf16),
            pltpu.VMEM((tok, groups * N), bf16),
            pltpu.VMEM((tok, width), bf16),
            pltpu.VMEM((2 * share, gw), bf16),
            pltpu.VMEM((groups, tok, 2 * share), bf16),
            pltpu.VMEM((groups, tok + 16, 2 * share), bf16),
            pltpu.VMEM((groups, gw // 128, 128), f32),
            pltpu.VMEM((groups, tok, N), bf16),
            pltpu.VMEM((groups, tok, N), bf16),
            pltpu.VMEM((CHUNKS, groups, tok, cw), bf16),
            pltpu.VMEM((groups, gw // 128, 128), f32),
            pltpu.VMEM((SLOTS, groups, N, cw), f32),
            pltpu.VMEM((CHUNKS, N, cw), f32),
            pltpu.VMEM((CHUNKS, 1, cw), f32),
            pltpu.VMEM((N, cw), f32),
            pltpu.VMEM((CHUNKS, N, cw), bf16),
            pltpu.VMEM((CHUNKS, 8, cw), f32),
            pltpu.VMEM((CHUNKS, N, cw), bf16),
            pltpu.VMEM((CHUNKS, 8, cw), f32),
            pltpu.VMEM((CHUNKS, N, cw), bf16),
            pltpu.VMEM((CHUNKS, N, cw), bf16),
            pltpu.VMEM((CHUNKS, groups, tok, cw), bf16),
            pltpu.VMEM((tok, width), bf16),
            pltpu.VMEM((tok, width), f32),
            dma((3,)),
            dma,
            dma,
            dma,
            dma((CHUNKS,)),
            dma((CHUNKS,)),
            dma((CHUNKS,)),
            dma((CHUNKS,)),
            dma((CHUNKS, 4)),
            dma,
            dma,
            dma,
            dma((CHUNKS,)),
            dma((CHUNKS, groups)),
            dma((CHUNKS,)),
            dma((CHUNKS,)),
            dma((CHUNKS,)),
        ],
        compiler_params=pltpu.CompilerParams(
            collective_id=0, has_side_effects=True, vmem_limit_bytes=56 * 1024 * 1024
        ),
    )(
        mixer_input,
        step_raw,
        b_proj,
        c_proj,
        step_bias.reshape(1, heads),
        decay_log.reshape(1, heads),
        skip_gain.reshape(1, heads),
    )


def solution(mesh):
    return jax.shard_map(
        body,
        mesh=mesh,
        in_specs=(
            P(("seq", "ctx"), None),
            P(("seq", "ctx"), None),
            P(("seq", "ctx"), None),
            P(("seq", "ctx"), None),
            P(),
            P(),
            P(),
        ),
        out_specs=P(("seq", "ctx"), None),
        check_vma=False,
    )
```

```python
import functools

import jax
import jax.numpy as jnp
from jax import lax
from jax.experimental import pallas as pl
from jax.experimental.pallas import tpu as pltpu
from jax.sharding import PartitionSpec as P

P_SIZE = 64
N = 256
CHUNKS = 8
SLOTS = 4


def scan_kernel(
    nc,
    ns,
    groups,
    x_hbm,
    step_hbm,
    b_hbm,
    c_hbm,
    bias_hbm,
    dlog_hbm,
    gain_hbm,
    o_ref,
    step_ref,
    bias_ref,
    dlog_ref,
    gain_ref,
    xv,
    bv,
    cv,
    xw,
    spread,
    w2,
    ec2,
    dsend,
    rb,
    rc,
    rx,
    rd,
    wide_d,
    states,
    total,
    whole,
    entry,
    pre,
    pre_d,
    run,
    run_d,
    head,
    nexthead,
    offs,
    offr,
    part,
    load_sem,
    sb_sem,
    sc_sem,
    sd_sem,
    sx_sem,
    so_sem,
    sr_sem,
    srd_sem,
    sh_sem,
    rb_sem,
    rc_sem,
    rd_sem,
    rx_sem,
    ro_sem,
    rr_sem,
    rrd_sem,
    rh_sem,
):
    f32, bf16 = jnp.float32, jnp.bfloat16
    me = lax.axis_index("ctx")
    sq = lax.axis_index("seq")
    tok, width = xv.shape
    heads = step_ref.shape[1]
    cw = width // groups // CHUNKS
    share = heads // groups
    gw = share * P_SIZE
    side = groups // 2
    half, span = lax.div(me, groups), lax.rem(me, groups)
    row, col = lax.div(span, side), lax.rem(span, side)
    flip = half * side
    mine = lax.rem(span + flip, groups)
    across = (1 - half) * groups + lax.rem(span + side, groups)
    role = lax.rem(sq, 2) * 2 + half
    block = lax.div(sq, 2)
    blocks = ns // 2
    inner_x = block < blocks - 1

    def partner(k):
        return lax.rem(row + lax.div(k, side), 2) * side + lax.rem(col + lax.rem(k, side), side)

    def source(k):
        return lax.rem(row + lax.div(k, side), 2) * side + lax.rem(
            col + side - lax.rem(k, side), side
        )

    def group_of(s):
        return lax.rem(s + flip, groups)

    def to_ctx(s):
        return {"ctx": half * groups + s}

    def following():
        return {"ctx": across, "seq": jnp.where(role == 1, sq + 1, sq)}

    def preceding():
        return {"ctx": across, "seq": jnp.where(role == 2, sq - 1, sq)}

    def carrier():
        return {
            "ctx": jnp.where(half == 1, me, across),
            "seq": 2 * block - 1,
        }

    def receiver(r):
        return {"ctx": me if r % 2 == 1 else across, "seq": 2 * block + 2 + r // 2}

    barrier = pltpu.get_barrier_semaphore()

    def greet(k, carry):
        pl.semaphore_signal(barrier, inc=1, device_id=to_ctx(partner(k)))
        return carry

    lax.fori_loop(1, groups, greet, 0)

    @pl.when(role > 0)
    def _():
        pl.semaphore_signal(barrier, inc=1, device_id=preceding())

    @pl.when(role < 3)
    def _():
        pl.semaphore_signal(barrier, inc=1, device_id=following())

    @pl.when(block > 0)
    def _():
        pl.semaphore_signal(barrier, inc=1, device_id=carrier())

    @pl.when((role == 3) & inner_x)
    def _():
        for r in range(4):
            pl.semaphore_signal(barrier, inc=1, device_id=receiver(r))

    loads = (
        pltpu.make_async_copy(x_hbm, xv, load_sem.at[0]),
        pltpu.make_async_copy(b_hbm, bv, load_sem.at[1]),
        pltpu.make_async_copy(c_hbm, cv, load_sem.at[2]),
        pltpu.make_async_copy(step_hbm, step_ref, load_sem.at[3]),
        pltpu.make_async_copy(bias_hbm, bias_ref, load_sem.at[4]),
        pltpu.make_async_copy(dlog_hbm, dlog_ref, load_sem.at[5]),
        pltpu.make_async_copy(gain_hbm, gain_ref, load_sem.at[6]),
    )
    for load in loads[3:] + loads[:3]:
        load.start()

    friends = (
        groups
        - 1
        + jnp.where(role > 0, 1, 0)
        + jnp.where(role < 3, 1, 0)
        + jnp.where(block > 0, 1, 0)
        + jnp.where((role == 3) & inner_x, 4, 0)
    )
    pl.semaphore_wait(barrier, friends)

    def columns(start, size):
        return pl.ds(pl.multiple_of(start, 128), size)

    def send_group(src, dst, send_sem, recv_sem):
        def one(k, carry):
            peer = partner(groups - k)
            pltpu.make_async_remote_copy(
                src_ref=src.at[:, columns(group_of(peer) * N, N)],
                dst_ref=dst.at[span],
                send_sem=send_sem,
                recv_sem=recv_sem,
                device_id=to_ctx(peer),
            ).start()
            return carry

        lax.fori_loop(1, groups, one, 0)

    def send_x(c):
        def one(k, carry):
            peer = partner(groups - k)
            pltpu.make_async_remote_copy(
                src_ref=xw.at[:, columns(group_of(peer) * gw + c * cw, cw)],
                dst_ref=rx.at[c, span],
                send_sem=sx_sem.at[c],
                recv_sem=rx_sem.at[c],
                device_id=to_ctx(peer),
            ).start()
            return carry

        lax.fori_loop(1, groups, one, 0)
        pltpu.make_async_copy(
            xw.at[:, columns(mine * gw + c * cw, cw)], rx.at[c, span], rx_sem.at[c]
        ).start()

    send_group(b_hbm, rb, sb_sem, rb_sem)

    for load in loads[3:]:
        load.wait()
    v = step_ref[...].astype(f32) + bias_ref[...]
    dt = jnp.maximum(v, 0.0) + jnp.log1p(jnp.exp(-jnp.abs(v)))
    rate = dt * (-jnp.exp(dlog_ref[...]))
    rows = lax.broadcasted_iota(jnp.int32, (tok, tok), 0)
    cols = lax.broadcasted_iota(jnp.int32, (tok, tok), 1)
    tri = (rows >= cols).astype(f32)
    cum = jnp.dot(tri, rate, precision=lax.Precision.HIGHEST, preferred_element_type=f32)
    w = dt * jnp.exp(-cum)
    ec = jnp.exp(cum)
    w_hi = w.astype(bf16)
    w_lo = (w - w_hi.astype(f32)).astype(bf16)
    e_hi = ec.astype(bf16)
    e_lo = (ec - e_hi.astype(f32)).astype(bf16)
    gain = jnp.broadcast_to(gain_ref[...], (16, heads))
    g_hi = gain.astype(bf16)
    g_lo = (gain - g_hi.astype(f32)).astype(bf16)
    dsend[...] = jnp.zeros(dsend.shape, f32)
    for g in range(groups):
        part_of = slice(g * share, (g + 1) * share)
        w2[g, :, :share] = w_hi[:, part_of]
        w2[g, :, share:] = w_lo[:, part_of]
        ec2[g, :tok, :share] = e_hi[:, part_of]
        ec2[g, :tok, share:] = e_lo[:, part_of]
        ec2[g, tok:, :share] = g_hi[:, part_of]
        ec2[g, tok:, share:] = g_lo[:, part_of]
        dsend[g, :, :share] = ec[tok - 1 :, part_of]
    slot_of = lax.broadcasted_iota(jnp.int32, (2 * share, gw), 0)
    lane_of = lax.broadcasted_iota(jnp.int32, (2 * share, gw), 1)
    spread[...] = jnp.where(lax.rem(slot_of, share) == lax.div(lane_of, P_SIZE), 1.0, 0.0).astype(bf16)

    loads[0].wait()

    def weigh(c):
        def one(g, carry):
            at = columns(g * gw + c * cw, cw)
            weight = jnp.dot(w2[g], spread[:, c * cw : (c + 1) * cw], preferred_element_type=f32)
            xw[:, at] = (xv[:, at].astype(f32) * weight).astype(bf16)
            return carry

        lax.fori_loop(0, groups, one, 0)

    weigh(0)
    send_x(0)

    def send_d(k, carry):
        peer = partner(groups - k)
        pltpu.make_async_remote_copy(
            src_ref=dsend.at[group_of(peer)],
            dst_ref=rd.at[span],
            send_sem=sd_sem,
            recv_sem=rd_sem,
            device_id=to_ctx(peer),
        ).start()
        return carry

    lax.fori_loop(1, groups, send_d, 0)
    pltpu.make_async_copy(dsend.at[mine], rd.at[span], rd_sem).start()
    for c in range(1, CHUNKS):
        weigh(c)
        send_x(c)
        if c == 4:
            send_group(c_hbm, rc, sc_sem, rc_sem)

    loads[1].wait()
    loads[2].wait()
    own = columns(mine * N, N)
    pltpu.make_async_copy(bv.at[:, own], rb.at[span], rb_sem).start()
    pltpu.make_async_copy(cv.at[:, own], rc.at[span], rc_sem).start()

    @pl.when(role == 0)
    def _():
        pre[...] = jnp.zeros(pre.shape, bf16)
        pre_d[...] = jnp.ones(pre_d.shape, f32)

    @pl.when(block == 0)
    def _():
        head[...] = jnp.zeros(head.shape, bf16)

    def local_part(g):
        at = slice(g * gw, (g + 1) * gw)
        state_at = slice(g * N, (g + 1) * N)
        inner = lax.dot_general(
            cv[:, state_at], bv[:, state_at], (((1,), (1,)), ((), ())), preferred_element_type=f32
        )
        inner = jnp.where(rows >= cols, inner, 0.0)
        top = inner.astype(bf16)
        rest = (inner - top.astype(f32)).astype(bf16)

        def one(c, carry):
            at = columns(g * gw + c * cw, cw)
            diag = jnp.dot(top, xw[:, at], preferred_element_type=f32)
            diag += jnp.dot(rest, xw[:, at], preferred_element_type=f32)
            scale = jnp.dot(ec2[g], spread[:, columns(c * cw, cw)], preferred_element_type=f32)
            part[:, at] = scale[:tok] * diag + scale[tok : tok + 1] * xv[:, at].astype(f32)
            return carry

        lax.fori_loop(0, CHUNKS, one, 0)

    def widen_decays():
        left = jnp.concatenate([rd[s] for s in range(groups)], axis=0)[:, :share]
        wide = jnp.zeros((groups, gw), f32)
        for _ in range(3):
            term = left.astype(bf16)
            left = left - term.astype(f32)
            wide = wide + jnp.dot(term, spread[:share], preferred_element_type=f32)
        for s in range(groups):
            wide_d[s] = wide[s : s + 1]

    def decay_row(c, s):
        return wide_d[s, :, c * cw : (c + 1) * cw]

    def gather_states(c):
        pltpu.make_async_copy(rx.at[c], rx.at[c], rx_sem.at[c]).wait()
        slot = c % SLOTS
        total[c] = jnp.zeros(total.shape[1:], f32)

        def one(s, product):
            piece = lax.dot_general(
                rb[s], rx[c, s], (((0,), (0,)), ((), ())), preferred_element_type=f32
            )
            factor = decay_row(c, s)
            states[slot, s] = piece
            total[c] = factor * (total[c] + piece)
            return product * factor

        whole[c] = lax.fori_loop(0, groups, one, jnp.ones((1, cw), f32))

    def pass_run(c):
        return (
            pltpu.make_async_remote_copy(
                src_ref=run.at[c],
                dst_ref=pre.at[c],
                send_sem=sr_sem.at[c],
                recv_sem=rr_sem.at[c],
                device_id=following(),
            ),
            pltpu.make_async_remote_copy(
                src_ref=run_d.at[c],
                dst_ref=pre_d.at[c],
                send_sem=srd_sem.at[c],
                recv_sem=rrd_sem.at[c],
                device_id=following(),
            ),
        )

    def pass_head(c, r):
        return pltpu.make_async_remote_copy(
            src_ref=nexthead.at[c],
            dst_ref=head.at[c],
            send_sem=sh_sem.at[c, r],
            recv_sem=rh_sem.at[c],
            device_id=receiver(r),
        )

    def compose(c):
        @pl.when(role > 0)
        def _():
            for copy in pass_run(c):
                copy.wait_recv()

        ahead = whole[c] * pre[c].astype(f32) + total[c]
        span_d = whole[c] * pre_d[c, :1]

        @pl.when(role < 3)
        def _():
            run[c] = ahead.astype(bf16)
            run_d[c] = jnp.broadcast_to(span_d, run_d.shape[1:])
            for copy in pass_run(c):
                copy.start()

        @pl.when((role == 3) & inner_x)
        def _():
            total[c] = ahead
            whole[c] = span_d

    def forward(c):
        @pl.when((role == 3) & inner_x)
        def _():
            @pl.when(block > 0)
            def _():
                pass_head(c, 0).wait_recv()

            nexthead[c] = (whole[c] * head[c].astype(f32) + total[c]).astype(bf16)
            for r in (3, 2, 1, 0):
                pass_head(c, r).start()

    def read_states(c):
        @pl.when((block > 0) & ((role < 3) | (block == blocks - 1)))
        def _():
            pass_head(c, 0).wait_recv()

        slot = c % SLOTS
        entry[...] = pre_d[c, :1] * head[c].astype(f32) + pre[c].astype(f32)

        def one(s, carry):
            state = entry[...]
            offs[c, s] = jnp.dot(rc[s], state.astype(bf16), preferred_element_type=f32).astype(bf16)
            entry[...] = decay_row(c, s) * (state + states[slot, s])
            return carry

        lax.fori_loop(0, groups, one, 0)
        at = columns(mine * gw + c * cw, cw)

        def send(k, carry):
            peer = partner(groups - k)
            pltpu.make_async_remote_copy(
                src_ref=offs.at[c, peer],
                dst_ref=offr.at[:, at],
                send_sem=so_sem.at[c],
                recv_sem=ro_sem.at[c, span],
                device_id=to_ctx(peer),
            ).start()
            return carry

        lax.fori_loop(1, groups, send, 0)
        pltpu.make_async_copy(offs.at[c, span], offr.at[:, at], ro_sem.at[c, span]).start()

    def combine(c):
        def one(k, carry):
            s = source(lax.rem(groups - k, groups))
            g = group_of(s)
            at = columns(g * gw + c * cw, cw)
            pltpu.make_async_copy(offs.at[c, 0], offr.at[:, at], ro_sem.at[c, s]).wait()
            scale = jnp.dot(
                ec2[g, :tok, :], spread[:, c * cw : (c + 1) * cw], preferred_element_type=f32
            )
            o_ref[:, at] = (part[:, at] + scale * offr[:, at].astype(f32)).astype(bf16)
            return carry

        lax.fori_loop(0, groups, one, 0)

    pltpu.make_async_copy(rb, rb, rb_sem).wait()
    pltpu.make_async_copy(rd, rd, rd_sem).wait()
    widen_decays()
    lag = SLOTS - 1
    for c in range(CHUNKS + lag):
        if c < CHUNKS:
            gather_states(c)
            compose(c)
            forward(c)
        if c == lag:
            pltpu.make_async_copy(rc, rc, rc_sem).wait()
        if c >= lag:
            read_states(c - lag)
        if c < groups:
            local_part(c)
    for c in range(CHUNKS):
        combine(c)

    for c in range(CHUNKS):
        pltpu.make_async_copy(rx.at[c, 1:], rx.at[c, 1:], sx_sem.at[c]).wait()
        pltpu.make_async_copy(offs.at[c, 1:], offs.at[c, 1:], so_sem.at[c]).wait()

        @pl.when(role < 3)
        def _():
            for copy in pass_run(c):
                copy.wait_send()

        @pl.when((role == 3) & inner_x)
        def _():
            for r in range(4):
                pass_head(c, r).wait_send()

    pltpu.make_async_copy(rb.at[1:], rb.at[1:], sb_sem).wait()
    pltpu.make_async_copy(rc.at[1:], rc.at[1:], sc_sem).wait()
    pltpu.make_async_copy(rd.at[1:], rd.at[1:], sd_sem).wait()


def body(mixer_input, step_raw, b_proj, c_proj, step_bias, decay_log, skip_gain):
    nc, ns = lax.axis_size("ctx"), lax.axis_size("seq")
    tok, width = mixer_input.shape
    heads = step_raw.shape[1]
    groups = b_proj.shape[1] // N
    share = heads // groups
    gw = share * P_SIZE
    cw = gw // CHUNKS
    f32, bf16 = jnp.float32, jnp.bfloat16
    any_spec = pl.BlockSpec(memory_space=pl.ANY)
    vmem_spec = pl.BlockSpec(memory_space=pltpu.VMEM)
    dma = pltpu.SemaphoreType.DMA
    return pl.pallas_call(
        functools.partial(scan_kernel, nc, ns, groups),
        out_shape=pltpu.VMEM((tok, width), bf16),
        in_specs=[any_spec] * 7,
        out_specs=vmem_spec,
        scratch_shapes=[
            pltpu.VMEM((tok, heads), bf16),
            pltpu.VMEM((1, heads), f32),
            pltpu.VMEM((1, heads), f32),
            pltpu.VMEM((1, heads), f32),
            pltpu.VMEM((tok, width), bf16),
            pltpu.VMEM((tok, groups * N), bf16),
            pltpu.VMEM((tok, groups * N), bf16),
            pltpu.VMEM((tok, width), bf16),
            pltpu.VMEM((2 * share, gw), bf16),
            pltpu.VMEM((groups, tok, 2 * share), bf16),
            pltpu.VMEM((groups, tok + 16, 2 * share), bf16),
            pltpu.VMEM((groups, 1, 128), f32),
            pltpu.VMEM((groups, tok, N), bf16),
            pltpu.VMEM((groups, tok, N), bf16),
            pltpu.VMEM((CHUNKS, groups, tok, cw), bf16),
            pltpu.VMEM((groups, 1, 128), f32),
            pltpu.VMEM((groups, 1, gw), f32),
            pltpu.VMEM((SLOTS, groups, N, cw), f32),
            pltpu.VMEM((CHUNKS, N, cw), f32),
            pltpu.VMEM((CHUNKS, 1, cw), f32),
            pltpu.VMEM((N, cw), f32),
            pltpu.VMEM((CHUNKS, N, cw), bf16),
            pltpu.VMEM((CHUNKS, 8, cw), f32),
            pltpu.VMEM((CHUNKS, N, cw), bf16),
            pltpu.VMEM((CHUNKS, 8, cw), f32),
            pltpu.VMEM((CHUNKS, N, cw), bf16),
            pltpu.VMEM((CHUNKS, N, cw), bf16),
            pltpu.VMEM((CHUNKS, groups, tok, cw), bf16),
            pltpu.VMEM((tok, width), bf16),
            pltpu.VMEM((tok, width), f32),
            dma((7,)),
            dma,
            dma,
            dma,
            dma((CHUNKS,)),
            dma((CHUNKS,)),
            dma((CHUNKS,)),
            dma((CHUNKS,)),
            dma((CHUNKS, 4)),
            dma,
            dma,
            dma,
            dma((CHUNKS,)),
            dma((CHUNKS, groups)),
            dma((CHUNKS,)),
            dma((CHUNKS,)),
            dma((CHUNKS,)),
        ],
        compiler_params=pltpu.CompilerParams(
            collective_id=0, has_side_effects=True, vmem_limit_bytes=56 * 1024 * 1024
        ),
    )(
        mixer_input,
        step_raw,
        b_proj,
        c_proj,
        step_bias.reshape(1, heads),
        decay_log.reshape(1, heads),
        skip_gain.reshape(1, heads),
    )


def solution(mesh):
    return jax.shard_map(
        body,
        mesh=mesh,
        in_specs=(
            P(("seq", "ctx"), None),
            P(("seq", "ctx"), None),
            P(("seq", "ctx"), None),
            P(("seq", "ctx"), None),
            P(),
            P(),
            P(),
        ),
        out_specs=P(("seq", "ctx"), None),
        check_vma=False,
    )
```

```python
import functools

import jax
import jax.numpy as jnp
from jax import lax
from jax.experimental import pallas as pl
from jax.experimental.pallas import tpu as pltpu
from jax.sharding import PartitionSpec as P

P_SIZE = 64
N = 256
CHUNKS = 8
SLOTS = 4


def scan_kernel(
    nc,
    ns,
    groups,
    x_hbm,
    step_hbm,
    b_hbm,
    c_hbm,
    bias_hbm,
    dlog_hbm,
    gain_hbm,
    o_ref,
    step_ref,
    bias_ref,
    dlog_ref,
    gain_ref,
    xv,
    bv,
    cv,
    xw,
    spread,
    w2,
    ec2,
    dsend,
    rb,
    rc,
    rx,
    rd,
    wide_d,
    states,
    total,
    whole,
    entry,
    pre,
    pre_d,
    run,
    run_d,
    head,
    nexthead,
    offs,
    offr,
    part,
    load_sem,
    sb_sem,
    sc_sem,
    sd_sem,
    sx_sem,
    so_sem,
    sr_sem,
    srd_sem,
    sh_sem,
    rb_sem,
    rc_sem,
    rd_sem,
    rx_sem,
    ro_sem,
    rr_sem,
    rrd_sem,
    rh_sem,
):
    f32, bf16 = jnp.float32, jnp.bfloat16
    me = lax.axis_index("ctx")
    sq = lax.axis_index("seq")
    tok, width = xv.shape
    heads = step_ref.shape[1]
    cw = width // groups // CHUNKS
    share = heads // groups
    gw = share * P_SIZE
    side = groups // 2
    half, span = lax.div(me, groups), lax.rem(me, groups)
    row, col = lax.div(span, side), lax.rem(span, side)
    flip = half * side
    mine = lax.rem(span + flip, groups)
    across = (1 - half) * groups + lax.rem(span + side, groups)
    role = lax.rem(sq, 2) * 2 + half
    block = lax.div(sq, 2)
    blocks = ns // 2
    inner_x = block < blocks - 1

    def partner(k):
        return lax.rem(row + lax.div(k, side), 2) * side + lax.rem(col + lax.rem(k, side), side)

    def source(k):
        return lax.rem(row + lax.div(k, side), 2) * side + lax.rem(
            col + side - lax.rem(k, side), side
        )

    def group_of(s):
        return lax.rem(s + flip, groups)

    def to_ctx(s):
        return {"ctx": half * groups + s}

    def following():
        return {"ctx": across, "seq": jnp.where(role == 1, sq + 1, sq)}

    def preceding():
        return {"ctx": across, "seq": jnp.where(role == 2, sq - 1, sq)}

    def carrier():
        return {
            "ctx": jnp.where(half == 1, me, across),
            "seq": 2 * block - 1,
        }

    def receiver(r):
        return {"ctx": me if r % 2 == 1 else across, "seq": 2 * block + 2 + r // 2}

    barrier = pltpu.get_barrier_semaphore()

    def greet(k, carry):
        pl.semaphore_signal(barrier, inc=1, device_id=to_ctx(partner(k)))
        return carry

    lax.fori_loop(1, groups, greet, 0)

    @pl.when(role > 0)
    def _():
        pl.semaphore_signal(barrier, inc=1, device_id=preceding())

    @pl.when(role < 3)
    def _():
        pl.semaphore_signal(barrier, inc=1, device_id=following())

    @pl.when(block > 0)
    def _():
        pl.semaphore_signal(barrier, inc=1, device_id=carrier())

    @pl.when((role == 3) & inner_x)
    def _():
        for r in range(4):
            pl.semaphore_signal(barrier, inc=1, device_id=receiver(r))

    loads = (
        pltpu.make_async_copy(x_hbm, xv, load_sem.at[0]),
        pltpu.make_async_copy(b_hbm, bv, load_sem.at[1]),
        pltpu.make_async_copy(c_hbm, cv, load_sem.at[2]),
        pltpu.make_async_copy(step_hbm, step_ref, load_sem.at[3]),
        pltpu.make_async_copy(bias_hbm, bias_ref, load_sem.at[4]),
        pltpu.make_async_copy(dlog_hbm, dlog_ref, load_sem.at[5]),
        pltpu.make_async_copy(gain_hbm, gain_ref, load_sem.at[6]),
    )
    for load in loads[3:] + loads[:3]:
        load.start()

    friends = (
        groups
        - 1
        + jnp.where(role > 0, 1, 0)
        + jnp.where(role < 3, 1, 0)
        + jnp.where(block > 0, 1, 0)
        + jnp.where((role == 3) & inner_x, 4, 0)
    )
    pl.semaphore_wait(barrier, friends)

    def columns(start, size):
        return pl.ds(pl.multiple_of(start, 128), size)

    def send_group(src, dst, send_sem, recv_sem):
        def one(k, carry):
            peer = partner(groups - k)
            pltpu.make_async_remote_copy(
                src_ref=src.at[:, columns(group_of(peer) * N, N)],
                dst_ref=dst.at[span],
                send_sem=send_sem,
                recv_sem=recv_sem,
                device_id=to_ctx(peer),
            ).start()
            return carry

        lax.fori_loop(1, groups, one, 0)

    def send_x(c):
        def one(k, carry):
            peer = partner(groups - k)
            pltpu.make_async_remote_copy(
                src_ref=xw.at[:, columns(group_of(peer) * gw + c * cw, cw)],
                dst_ref=rx.at[c, span],
                send_sem=sx_sem.at[c],
                recv_sem=rx_sem.at[c],
                device_id=to_ctx(peer),
            ).start()
            return carry

        lax.fori_loop(1, groups, one, 0)
        pltpu.make_async_copy(
            xw.at[:, columns(mine * gw + c * cw, cw)], rx.at[c, span], rx_sem.at[c]
        ).start()

    send_group(b_hbm, rb, sb_sem, rb_sem)

    for load in loads[3:]:
        load.wait()
    v = step_ref[...].astype(f32) + bias_ref[...]
    dt = jnp.maximum(v, 0.0) + jnp.log1p(jnp.exp(-jnp.abs(v)))
    rate = dt * (-jnp.exp(dlog_ref[...]))
    rows = lax.broadcasted_iota(jnp.int32, (tok, tok), 0)
    cols = lax.broadcasted_iota(jnp.int32, (tok, tok), 1)
    tri = (rows >= cols).astype(f32)
    cum = jnp.dot(tri, rate, precision=lax.Precision.HIGHEST, preferred_element_type=f32)
    w = dt * jnp.exp(-cum)
    ec = jnp.exp(cum)
    w_hi = w.astype(bf16)
    w_lo = (w - w_hi.astype(f32)).astype(bf16)
    e_hi = ec.astype(bf16)
    e_lo = (ec - e_hi.astype(f32)).astype(bf16)
    gain = jnp.broadcast_to(gain_ref[...], (16, heads))
    g_hi = gain.astype(bf16)
    g_lo = (gain - g_hi.astype(f32)).astype(bf16)
    dsend[...] = jnp.zeros(dsend.shape, f32)
    for g in range(groups):
        part_of = slice(g * share, (g + 1) * share)
        w2[g, :, :share] = w_hi[:, part_of]
        w2[g, :, share:] = w_lo[:, part_of]
        ec2[g, :tok, :share] = e_hi[:, part_of]
        ec2[g, :tok, share:] = e_lo[:, part_of]
        ec2[g, tok:, :share] = g_hi[:, part_of]
        ec2[g, tok:, share:] = g_lo[:, part_of]
        dsend[g, :, :share] = ec[tok - 1 :, part_of]
    slot_of = lax.broadcasted_iota(jnp.int32, (2 * share, gw), 0)
    lane_of = lax.broadcasted_iota(jnp.int32, (2 * share, gw), 1)
    spread[...] = jnp.where(lax.rem(slot_of, share) == lax.div(lane_of, P_SIZE), 1.0, 0.0).astype(bf16)

    loads[0].wait()

    def weigh(c):
        def one(g, carry):
            at = columns(g * gw + c * cw, cw)
            weight = jnp.dot(w2[g], spread[:, c * cw : (c + 1) * cw], preferred_element_type=f32)
            xw[:, at] = (xv[:, at].astype(f32) * weight).astype(bf16)
            return carry

        lax.fori_loop(0, groups, one, 0)

    weigh(0)
    send_x(0)

    def send_d(k, carry):
        peer = partner(groups - k)
        pltpu.make_async_remote_copy(
            src_ref=dsend.at[group_of(peer)],
            dst_ref=rd.at[span],
            send_sem=sd_sem,
            recv_sem=rd_sem,
            device_id=to_ctx(peer),
        ).start()
        return carry

    lax.fori_loop(1, groups, send_d, 0)
    pltpu.make_async_copy(dsend.at[mine], rd.at[span], rd_sem).start()
    for c in range(1, CHUNKS):
        weigh(c)
        send_x(c)
        if c == 4:
            send_group(c_hbm, rc, sc_sem, rc_sem)

    loads[1].wait()
    loads[2].wait()
    own = columns(mine * N, N)
    pltpu.make_async_copy(bv.at[:, own], rb.at[span], rb_sem).start()
    pltpu.make_async_copy(cv.at[:, own], rc.at[span], rc_sem).start()

    @pl.when(role == 0)
    def _():
        pre[...] = jnp.zeros(pre.shape, bf16)
        pre_d[...] = jnp.ones(pre_d.shape, f32)

    @pl.when(block == 0)
    def _():
        head[...] = jnp.zeros(head.shape, bf16)

    def local_part(g):
        at = slice(g * gw, (g + 1) * gw)
        state_at = slice(g * N, (g + 1) * N)
        inner = lax.dot_general(
            cv[:, state_at], bv[:, state_at], (((1,), (1,)), ((), ())), preferred_element_type=f32
        )
        inner = jnp.where(rows >= cols, inner, 0.0)
        top = inner.astype(bf16)
        rest = (inner - top.astype(f32)).astype(bf16)

        def one(c, carry):
            at = columns(g * gw + c * cw, cw)
            diag = jnp.dot(top, xw[:, at], preferred_element_type=f32)
            diag += jnp.dot(rest, xw[:, at], preferred_element_type=f32)
            scale = jnp.dot(ec2[g], spread[:, columns(c * cw, cw)], preferred_element_type=f32)
            part[:, at] = scale[:tok] * diag + scale[tok : tok + 1] * xv[:, at].astype(f32)
            return carry

        lax.fori_loop(0, CHUNKS, one, 0)

    def widen_decays():
        left = jnp.concatenate([rd[s] for s in range(groups)], axis=0)[:, :share]
        wide = jnp.zeros((groups, gw), f32)
        for _ in range(3):
            term = left.astype(bf16)
            left = left - term.astype(f32)
            wide = wide + jnp.dot(term, spread[:share], preferred_element_type=f32)
        for s in range(groups):
            wide_d[s] = wide[s : s + 1]

    def decay_row(c, s):
        return wide_d[s, :, c * cw : (c + 1) * cw]

    def gather_states(c):
        pltpu.make_async_copy(rx.at[c], rx.at[c], rx_sem.at[c]).wait()
        slot = c % SLOTS
        total[c] = jnp.zeros(total.shape[1:], f32)

        def one(s, product):
            piece = lax.dot_general(
                rb[s], rx[c, s], (((0,), (0,)), ((), ())), preferred_element_type=f32
            )
            factor = decay_row(c, s)
            states[slot, s] = piece
            total[c] = factor * (total[c] + piece)
            return product * factor

        whole[c] = lax.fori_loop(0, groups, one, jnp.ones((1, cw), f32))

    def pass_run(c):
        return (
            pltpu.make_async_remote_copy(
                src_ref=run.at[c],
                dst_ref=pre.at[c],
                send_sem=sr_sem.at[c],
                recv_sem=rr_sem.at[c],
                device_id=following(),
            ),
            pltpu.make_async_remote_copy(
                src_ref=run_d.at[c],
                dst_ref=pre_d.at[c],
                send_sem=srd_sem.at[c],
                recv_sem=rrd_sem.at[c],
                device_id=following(),
            ),
        )

    def pass_head(c, r):
        return pltpu.make_async_remote_copy(
            src_ref=nexthead.at[c],
            dst_ref=head.at[c],
            send_sem=sh_sem.at[c, r],
            recv_sem=rh_sem.at[c],
            device_id=receiver(r),
        )

    def compose(c):
        @pl.when(role > 0)
        def _():
            pltpu.make_async_copy(pre.at[c], pre.at[c], rr_sem.at[c]).wait()
            pltpu.make_async_copy(pre_d.at[c], pre_d.at[c], rrd_sem.at[c]).wait()

        ahead = whole[c] * pre[c].astype(f32) + total[c]
        span_d = whole[c] * pre_d[c, :1]

        @pl.when(role < 3)
        def _():
            run[c] = ahead.astype(bf16)
            run_d[c] = jnp.broadcast_to(span_d, run_d.shape[1:])
            for copy in pass_run(c):
                copy.start()

        @pl.when((role == 3) & inner_x)
        def _():
            total[c] = ahead
            whole[c] = span_d

    def forward(c):
        @pl.when((role == 3) & inner_x)
        def _():
            @pl.when(block > 0)
            def _():
                pltpu.make_async_copy(head.at[c], head.at[c], rh_sem.at[c]).wait()

            nexthead[c] = (whole[c] * head[c].astype(f32) + total[c]).astype(bf16)
            for r in (3, 2, 1, 0):
                pass_head(c, r).start()

    def read_states(c):
        @pl.when((block > 0) & ((role < 3) | (block == blocks - 1)))
        def _():
            pltpu.make_async_copy(head.at[c], head.at[c], rh_sem.at[c]).wait()

        slot = c % SLOTS
        entry[...] = pre_d[c, :1] * head[c].astype(f32) + pre[c].astype(f32)

        def one(s, carry):
            state = entry[...]
            offs[c, s] = jnp.dot(rc[s], state.astype(bf16), preferred_element_type=f32).astype(bf16)
            entry[...] = decay_row(c, s) * (state + states[slot, s])
            return carry

        lax.fori_loop(0, groups, one, 0)
        at = columns(mine * gw + c * cw, cw)

        def send(k, carry):
            peer = partner(groups - k)
            pltpu.make_async_remote_copy(
                src_ref=offs.at[c, peer],
                dst_ref=offr.at[:, at],
                send_sem=so_sem.at[c],
                recv_sem=ro_sem.at[c, span],
                device_id=to_ctx(peer),
            ).start()
            return carry

        lax.fori_loop(1, groups, send, 0)
        pltpu.make_async_copy(offs.at[c, span], offr.at[:, at], ro_sem.at[c, span]).start()

    def combine(c):
        def one(k, carry):
            s = source(lax.rem(groups - k, groups))
            g = group_of(s)
            at = columns(g * gw + c * cw, cw)
            pltpu.make_async_copy(offs.at[c, 0], offr.at[:, at], ro_sem.at[c, s]).wait()
            scale = jnp.dot(
                ec2[g, :tok, :], spread[:, c * cw : (c + 1) * cw], preferred_element_type=f32
            )
            o_ref[:, at] = (part[:, at] + scale * offr[:, at].astype(f32)).astype(bf16)
            return carry

        lax.fori_loop(0, groups, one, 0)

    pltpu.make_async_copy(rb, rb, rb_sem).wait()
    pltpu.make_async_copy(rd, rd, rd_sem).wait()
    widen_decays()
    lag = SLOTS - 1
    for c in range(CHUNKS + lag):
        if c < CHUNKS:
            gather_states(c)
            compose(c)
            forward(c)
        if c == lag:
            pltpu.make_async_copy(rc, rc, rc_sem).wait()
        if c >= lag:
            read_states(c - lag)
        if c < groups:
            local_part(c)
    for c in range(CHUNKS):
        combine(c)

    for c in range(CHUNKS):
        pltpu.make_async_copy(rx.at[c, 1:], rx.at[c, 1:], sx_sem.at[c]).wait()
        pltpu.make_async_copy(offs.at[c, 1:], offs.at[c, 1:], so_sem.at[c]).wait()

        @pl.when(role < 3)
        def _():
            for copy in pass_run(c):
                copy.wait_send()

        @pl.when((role == 3) & inner_x)
        def _():
            for r in range(4):
                pass_head(c, r).wait_send()

    pltpu.make_async_copy(rb.at[1:], rb.at[1:], sb_sem).wait()
    pltpu.make_async_copy(rc.at[1:], rc.at[1:], sc_sem).wait()
    pltpu.make_async_copy(rd.at[1:], rd.at[1:], sd_sem).wait()


def body(mixer_input, step_raw, b_proj, c_proj, step_bias, decay_log, skip_gain):
    nc, ns = lax.axis_size("ctx"), lax.axis_size("seq")
    tok, width = mixer_input.shape
    heads = step_raw.shape[1]
    groups = b_proj.shape[1] // N
    share = heads // groups
    gw = share * P_SIZE
    cw = gw // CHUNKS
    f32, bf16 = jnp.float32, jnp.bfloat16
    any_spec = pl.BlockSpec(memory_space=pl.ANY)
    vmem_spec = pl.BlockSpec(memory_space=pltpu.VMEM)
    dma = pltpu.SemaphoreType.DMA
    return pl.pallas_call(
        functools.partial(scan_kernel, nc, ns, groups),
        out_shape=pltpu.VMEM((tok, width), bf16),
        in_specs=[any_spec] * 7,
        out_specs=vmem_spec,
        scratch_shapes=[
            pltpu.VMEM((tok, heads), bf16),
            pltpu.VMEM((1, heads), f32),
            pltpu.VMEM((1, heads), f32),
            pltpu.VMEM((1, heads), f32),
            pltpu.VMEM((tok, width), bf16),
            pltpu.VMEM((tok, groups * N), bf16),
            pltpu.VMEM((tok, groups * N), bf16),
            pltpu.VMEM((tok, width), bf16),
            pltpu.VMEM((2 * share, gw), bf16),
            pltpu.VMEM((groups, tok, 2 * share), bf16),
            pltpu.VMEM((groups, tok + 16, 2 * share), bf16),
            pltpu.VMEM((groups, 1, 128), f32),
            pltpu.VMEM((groups, tok, N), bf16),
            pltpu.VMEM((groups, tok, N), bf16),
            pltpu.VMEM((CHUNKS, groups, tok, cw), bf16),
            pltpu.VMEM((groups, 1, 128), f32),
            pltpu.VMEM((groups, 1, gw), f32),
            pltpu.VMEM((SLOTS, groups, N, cw), f32),
            pltpu.VMEM((CHUNKS, N, cw), f32),
            pltpu.VMEM((CHUNKS, 1, cw), f32),
            pltpu.VMEM((N, cw), f32),
            pltpu.VMEM((CHUNKS, N, cw), bf16),
            pltpu.VMEM((CHUNKS, 8, cw), f32),
            pltpu.VMEM((CHUNKS, N, cw), bf16),
            pltpu.VMEM((CHUNKS, 8, cw), f32),
            pltpu.VMEM((CHUNKS, N, cw), bf16),
            pltpu.VMEM((CHUNKS, N, cw), bf16),
            pltpu.VMEM((CHUNKS, groups, tok, cw), bf16),
            pltpu.VMEM((tok, width), bf16),
            pltpu.VMEM((tok, width), f32),
            dma((7,)),
            dma,
            dma,
            dma,
            dma((CHUNKS,)),
            dma((CHUNKS,)),
            dma((CHUNKS,)),
            dma((CHUNKS,)),
            dma((CHUNKS, 4)),
            dma,
            dma,
            dma,
            dma((CHUNKS,)),
            dma((CHUNKS, groups)),
            dma((CHUNKS,)),
            dma((CHUNKS,)),
            dma((CHUNKS,)),
        ],
        compiler_params=pltpu.CompilerParams(
            collective_id=0, has_side_effects=True, vmem_limit_bytes=56 * 1024 * 1024
        ),
    )(
        mixer_input,
        step_raw,
        b_proj,
        c_proj,
        step_bias.reshape(1, heads),
        decay_log.reshape(1, heads),
        skip_gain.reshape(1, heads),
    )


def solution(mesh):
    return jax.shard_map(
        body,
        mesh=mesh,
        in_specs=(
            P(("seq", "ctx"), None),
            P(("seq", "ctx"), None),
            P(("seq", "ctx"), None),
            P(("seq", "ctx"), None),
            P(),
            P(),
            P(),
        ),
        out_specs=P(("seq", "ctx"), None),
        check_vma=False,
    )
```

```python
import functools

import jax
import jax.numpy as jnp
from jax import lax
from jax.experimental import pallas as pl
from jax.experimental.pallas import tpu as pltpu
from jax.sharding import PartitionSpec as P

P_SIZE = 64
N = 256
CHUNKS = 8
SLOTS = 4


def scan_kernel(
    nc,
    ns,
    groups,
    x_hbm,
    step_hbm,
    b_hbm,
    c_hbm,
    bias_hbm,
    dlog_hbm,
    gain_hbm,
    o_ref,
    step_ref,
    bias_ref,
    dlog_ref,
    gain_ref,
    xv,
    bv,
    cv,
    xw,
    spread,
    w2,
    ec2,
    dsend,
    rb,
    rc,
    rx,
    rd,
    wide_d,
    states,
    total,
    whole,
    entry,
    pre,
    pre_d,
    run,
    run_d,
    head,
    nexthead,
    offs,
    offr,
    part,
    load_sem,
    sb_sem,
    sc_sem,
    sd_sem,
    sx_sem,
    so_sem,
    sr_sem,
    srd_sem,
    sh_sem,
    rb_sem,
    rc_sem,
    rd_sem,
    rx_sem,
    ro_sem,
    rr_sem,
    rrd_sem,
    rh_sem,
):
    f32, bf16 = jnp.float32, jnp.bfloat16
    me = lax.axis_index("ctx")
    sq = lax.axis_index("seq")
    tok, width = xv.shape
    heads = step_ref.shape[1]
    cw = width // groups // CHUNKS
    share = heads // groups
    gw = share * P_SIZE
    side = groups // 2
    half, span = lax.div(me, groups), lax.rem(me, groups)
    row, col = lax.div(span, side), lax.rem(span, side)
    flip = half * side
    mine = lax.rem(span + flip, groups)
    across = (1 - half) * groups + lax.rem(span + side, groups)
    role = lax.rem(sq, 2) * 2 + half
    block = lax.div(sq, 2)
    blocks = ns // 2
    inner_x = block < blocks - 1

    def partner(k):
        return lax.rem(row + lax.div(k, side), 2) * side + lax.rem(col + lax.rem(k, side), side)

    def source(k):
        return lax.rem(row + lax.div(k, side), 2) * side + lax.rem(
            col + side - lax.rem(k, side), side
        )

    def group_of(s):
        return lax.rem(s + flip, groups)

    def to_ctx(s):
        return {"ctx": half * groups + s}

    def following():
        return {"ctx": across, "seq": jnp.where(role == 1, sq + 1, sq)}

    def preceding():
        return {"ctx": across, "seq": jnp.where(role == 2, sq - 1, sq)}

    def carrier():
        return {
            "ctx": jnp.where(half == 1, me, across),
            "seq": 2 * block - 1,
        }

    def receiver(r):
        return {"ctx": me if r % 2 == 1 else across, "seq": 2 * block + 2 + r // 2}

    barrier = pltpu.get_barrier_semaphore()

    def greet(k, carry):
        pl.semaphore_signal(barrier, inc=1, device_id=to_ctx(partner(k)))
        return carry

    lax.fori_loop(1, groups, greet, 0)

    @pl.when(role > 0)
    def _():
        pl.semaphore_signal(barrier, inc=1, device_id=preceding())

    @pl.when(role < 3)
    def _():
        pl.semaphore_signal(barrier, inc=1, device_id=following())

    @pl.when(block > 0)
    def _():
        pl.semaphore_signal(barrier, inc=1, device_id=carrier())

    @pl.when((role == 3) & inner_x)
    def _():
        for r in range(4):
            pl.semaphore_signal(barrier, inc=1, device_id=receiver(r))

    loads = (
        pltpu.make_async_copy(x_hbm, xv, load_sem.at[0]),
        pltpu.make_async_copy(b_hbm, bv, load_sem.at[1]),
        pltpu.make_async_copy(c_hbm, cv, load_sem.at[2]),
        pltpu.make_async_copy(step_hbm, step_ref, load_sem.at[3]),
        pltpu.make_async_copy(bias_hbm, bias_ref, load_sem.at[4]),
        pltpu.make_async_copy(dlog_hbm, dlog_ref, load_sem.at[5]),
        pltpu.make_async_copy(gain_hbm, gain_ref, load_sem.at[6]),
    )
    for load in loads[3:] + loads[:3]:
        load.start()

    friends = (
        groups
        - 1
        + jnp.where(role > 0, 1, 0)
        + jnp.where(role < 3, 1, 0)
        + jnp.where(block > 0, 1, 0)
        + jnp.where((role == 3) & inner_x, 4, 0)
    )
    pl.semaphore_wait(barrier, friends)

    def columns(start, size):
        return pl.ds(pl.multiple_of(start, 128), size)

    def send_group(src, dst, send_sem, recv_sem):
        def one(k, carry):
            peer = partner(groups - k)
            pltpu.make_async_remote_copy(
                src_ref=src.at[:, columns(group_of(peer) * N, N)],
                dst_ref=dst.at[span],
                send_sem=send_sem,
                recv_sem=recv_sem,
                device_id=to_ctx(peer),
            ).start()
            return carry

        lax.fori_loop(1, groups, one, 0)

    def send_x(c):
        def one(k, carry):
            peer = partner(groups - k)
            pltpu.make_async_remote_copy(
                src_ref=xw.at[:, columns(group_of(peer) * gw + c * cw, cw)],
                dst_ref=rx.at[c, span],
                send_sem=sx_sem.at[c],
                recv_sem=rx_sem.at[c],
                device_id=to_ctx(peer),
            ).start()
            return carry

        lax.fori_loop(1, groups, one, 0)
        pltpu.make_async_copy(
            xw.at[:, columns(mine * gw + c * cw, cw)], rx.at[c, span], rx_sem.at[c]
        ).start()

    send_group(b_hbm, rb, sb_sem, rb_sem)

    for load in loads[3:]:
        load.wait()
    v = step_ref[...].astype(f32) + bias_ref[...]
    dt = jnp.maximum(v, 0.0) + jnp.log1p(jnp.exp(-jnp.abs(v)))
    rate = dt * (-jnp.exp(dlog_ref[...]))
    rows = lax.broadcasted_iota(jnp.int32, (tok, tok), 0)
    cols = lax.broadcasted_iota(jnp.int32, (tok, tok), 1)
    tri = (rows >= cols).astype(f32)
    cum = jnp.dot(tri, rate, precision=lax.Precision.HIGHEST, preferred_element_type=f32)
    w = dt * jnp.exp(-cum)
    ec = jnp.exp(cum)
    w_hi = w.astype(bf16)
    w_lo = (w - w_hi.astype(f32)).astype(bf16)
    e_hi = ec.astype(bf16)
    e_lo = (ec - e_hi.astype(f32)).astype(bf16)
    gain = jnp.broadcast_to(gain_ref[...], (16, heads))
    g_hi = gain.astype(bf16)
    g_lo = (gain - g_hi.astype(f32)).astype(bf16)
    dsend[...] = jnp.zeros(dsend.shape, f32)
    for g in range(groups):
        part_of = slice(g * share, (g + 1) * share)
        w2[g, :, :share] = w_hi[:, part_of]
        w2[g, :, share:] = w_lo[:, part_of]
        ec2[g, :tok, :share] = e_hi[:, part_of]
        ec2[g, :tok, share:] = e_lo[:, part_of]
        ec2[g, tok:, :share] = g_hi[:, part_of]
        ec2[g, tok:, share:] = g_lo[:, part_of]
        dsend[g, :, :share] = ec[tok - 1 :, part_of]
    slot_of = lax.broadcasted_iota(jnp.int32, (2 * share, gw), 0)
    lane_of = lax.broadcasted_iota(jnp.int32, (2 * share, gw), 1)
    spread[...] = jnp.where(lax.rem(slot_of, share) == lax.div(lane_of, P_SIZE), 1.0, 0.0).astype(bf16)

    loads[0].wait()

    def weigh(c):
        def one(g, carry):
            at = columns(g * gw + c * cw, cw)
            weight = jnp.dot(w2[g], spread[:, c * cw : (c + 1) * cw], preferred_element_type=f32)
            xw[:, at] = (xv[:, at].astype(f32) * weight).astype(bf16)
            return carry

        lax.fori_loop(0, groups, one, 0)

    weigh(0)
    send_x(0)

    def send_d(k, carry):
        peer = partner(groups - k)
        pltpu.make_async_remote_copy(
            src_ref=dsend.at[group_of(peer)],
            dst_ref=rd.at[span],
            send_sem=sd_sem,
            recv_sem=rd_sem,
            device_id=to_ctx(peer),
        ).start()
        return carry

    lax.fori_loop(1, groups, send_d, 0)
    pltpu.make_async_copy(dsend.at[mine], rd.at[span], rd_sem).start()
    for c in range(1, CHUNKS):
        weigh(c)
        send_x(c)
        if c == 3:
            send_group(c_hbm, rc, sc_sem, rc_sem)

    loads[1].wait()
    loads[2].wait()
    own = columns(mine * N, N)
    pltpu.make_async_copy(bv.at[:, own], rb.at[span], rb_sem).start()
    pltpu.make_async_copy(cv.at[:, own], rc.at[span], rc_sem).start()

    @pl.when(role == 0)
    def _():
        pre[...] = jnp.zeros(pre.shape, bf16)
        pre_d[...] = jnp.ones(pre_d.shape, f32)

    @pl.when(block == 0)
    def _():
        head[...] = jnp.zeros(head.shape, bf16)

    def local_part(g):
        at = slice(g * gw, (g + 1) * gw)
        state_at = slice(g * N, (g + 1) * N)
        inner = lax.dot_general(
            cv[:, state_at], bv[:, state_at], (((1,), (1,)), ((), ())), preferred_element_type=f32
        )
        inner = jnp.where(rows >= cols, inner, 0.0)
        top = inner.astype(bf16)
        rest = (inner - top.astype(f32)).astype(bf16)

        def one(c, carry):
            at = columns(g * gw + c * cw, cw)
            diag = jnp.dot(top, xw[:, at], preferred_element_type=f32)
            diag += jnp.dot(rest, xw[:, at], preferred_element_type=f32)
            scale = jnp.dot(ec2[g], spread[:, columns(c * cw, cw)], preferred_element_type=f32)
            part[:, at] = scale[:tok] * diag + scale[tok : tok + 1] * xv[:, at].astype(f32)
            return carry

        lax.fori_loop(0, CHUNKS, one, 0)

    def widen_decays():
        left = jnp.concatenate([rd[s] for s in range(groups)], axis=0)[:, :share]
        wide = jnp.zeros((groups, gw), f32)
        for _ in range(3):
            term = left.astype(bf16)
            left = left - term.astype(f32)
            wide = wide + jnp.dot(term, spread[:share], preferred_element_type=f32)
        for s in range(groups):
            wide_d[s] = wide[s : s + 1]

    def decay_row(c, s):
        return wide_d[s, :, c * cw : (c + 1) * cw]

    def gather_states(c):
        pltpu.make_async_copy(rx.at[c], rx.at[c], rx_sem.at[c]).wait()
        slot = c % SLOTS
        total[c] = jnp.zeros(total.shape[1:], f32)

        def one(s, product):
            piece = lax.dot_general(
                rb[s], rx[c, s], (((0,), (0,)), ((), ())), preferred_element_type=f32
            )
            factor = decay_row(c, s)
            states[slot, s] = piece
            total[c] = factor * (total[c] + piece)
            return product * factor

        whole[c] = lax.fori_loop(0, groups, one, jnp.ones((1, cw), f32))

    def pass_run(c):
        return (
            pltpu.make_async_remote_copy(
                src_ref=run.at[c],
                dst_ref=pre.at[c],
                send_sem=sr_sem.at[c],
                recv_sem=rr_sem.at[c],
                device_id=following(),
            ),
            pltpu.make_async_remote_copy(
                src_ref=run_d.at[c],
                dst_ref=pre_d.at[c],
                send_sem=srd_sem.at[c],
                recv_sem=rrd_sem.at[c],
                device_id=following(),
            ),
        )

    def pass_head(c, r):
        return pltpu.make_async_remote_copy(
            src_ref=nexthead.at[c],
            dst_ref=head.at[c],
            send_sem=sh_sem.at[c, r],
            recv_sem=rh_sem.at[c],
            device_id=receiver(r),
        )

    def compose(c):
        @pl.when(role > 0)
        def _():
            pltpu.make_async_copy(pre.at[c], pre.at[c], rr_sem.at[c]).wait()
            pltpu.make_async_copy(pre_d.at[c], pre_d.at[c], rrd_sem.at[c]).wait()

        ahead = whole[c] * pre[c].astype(f32) + total[c]
        span_d = whole[c] * pre_d[c, :1]

        @pl.when(role < 3)
        def _():
            run[c] = ahead.astype(bf16)
            run_d[c] = jnp.broadcast_to(span_d, run_d.shape[1:])
            for copy in pass_run(c):
                copy.start()

        @pl.when((role == 3) & inner_x)
        def _():
            total[c] = ahead
            whole[c] = span_d

    def forward(c):
        @pl.when((role == 3) & inner_x)
        def _():
            @pl.when(block > 0)
            def _():
                pltpu.make_async_copy(head.at[c], head.at[c], rh_sem.at[c]).wait()

            nexthead[c] = (whole[c] * head[c].astype(f32) + total[c]).astype(bf16)
            for r in (3, 2, 1, 0):
                pass_head(c, r).start()

    def read_states(c):
        @pl.when((block > 0) & ((role < 3) | (block == blocks - 1)))
        def _():
            pltpu.make_async_copy(head.at[c], head.at[c], rh_sem.at[c]).wait()

        slot = c % SLOTS
        entry[...] = pre_d[c, :1] * head[c].astype(f32) + pre[c].astype(f32)

        def one(s, carry):
            state = entry[...]
            offs[c, s] = jnp.dot(rc[s], state.astype(bf16), preferred_element_type=f32).astype(bf16)
            entry[...] = decay_row(c, s) * (state + states[slot, s])
            return carry

        lax.fori_loop(0, groups, one, 0)
        at = columns(mine * gw + c * cw, cw)

        def send(k, carry):
            peer = partner(groups - k)
            pltpu.make_async_remote_copy(
                src_ref=offs.at[c, peer],
                dst_ref=offr.at[:, at],
                send_sem=so_sem.at[c],
                recv_sem=ro_sem.at[c, span],
                device_id=to_ctx(peer),
            ).start()
            return carry

        lax.fori_loop(1, groups, send, 0)
        pltpu.make_async_copy(offs.at[c, span], offr.at[:, at], ro_sem.at[c, span]).start()

    def combine(c):
        def one(k, carry):
            s = source(lax.rem(groups - k, groups))
            g = group_of(s)
            at = columns(g * gw + c * cw, cw)
            pltpu.make_async_copy(offs.at[c, 0], offr.at[:, at], ro_sem.at[c, s]).wait()
            scale = jnp.dot(
                ec2[g, :tok, :], spread[:, c * cw : (c + 1) * cw], preferred_element_type=f32
            )
            o_ref[:, at] = (part[:, at] + scale * offr[:, at].astype(f32)).astype(bf16)
            return carry

        lax.fori_loop(0, groups, one, 0)

    pltpu.make_async_copy(rb, rb, rb_sem).wait()
    pltpu.make_async_copy(rd, rd, rd_sem).wait()
    widen_decays()
    lag = SLOTS - 1
    for c in range(CHUNKS + lag):
        if c < CHUNKS:
            gather_states(c)
            compose(c)
            forward(c)
        if c == lag:
            pltpu.make_async_copy(rc, rc, rc_sem).wait()
        if c >= lag:
            read_states(c - lag)
        if c < groups:
            local_part(c)
    for c in range(CHUNKS):
        combine(c)

    for c in range(CHUNKS):
        pltpu.make_async_copy(rx.at[c, 1:], rx.at[c, 1:], sx_sem.at[c]).wait()
        pltpu.make_async_copy(offs.at[c, 1:], offs.at[c, 1:], so_sem.at[c]).wait()

        @pl.when(role < 3)
        def _():
            for copy in pass_run(c):
                copy.wait_send()

        @pl.when((role == 3) & inner_x)
        def _():
            for r in range(4):
                pass_head(c, r).wait_send()

    pltpu.make_async_copy(rb.at[1:], rb.at[1:], sb_sem).wait()
    pltpu.make_async_copy(rc.at[1:], rc.at[1:], sc_sem).wait()
    pltpu.make_async_copy(rd.at[1:], rd.at[1:], sd_sem).wait()


def body(mixer_input, step_raw, b_proj, c_proj, step_bias, decay_log, skip_gain):
    nc, ns = lax.axis_size("ctx"), lax.axis_size("seq")
    tok, width = mixer_input.shape
    heads = step_raw.shape[1]
    groups = b_proj.shape[1] // N
    share = heads // groups
    gw = share * P_SIZE
    cw = gw // CHUNKS
    f32, bf16 = jnp.float32, jnp.bfloat16
    any_spec = pl.BlockSpec(memory_space=pl.ANY)
    vmem_spec = pl.BlockSpec(memory_space=pltpu.VMEM)
    dma = pltpu.SemaphoreType.DMA
    return pl.pallas_call(
        functools.partial(scan_kernel, nc, ns, groups),
        out_shape=pltpu.VMEM((tok, width), bf16),
        in_specs=[any_spec] * 7,
        out_specs=vmem_spec,
        scratch_shapes=[
            pltpu.VMEM((tok, heads), bf16),
            pltpu.VMEM((1, heads), f32),
            pltpu.VMEM((1, heads), f32),
            pltpu.VMEM((1, heads), f32),
            pltpu.VMEM((tok, width), bf16),
            pltpu.VMEM((tok, groups * N), bf16),
            pltpu.VMEM((tok, groups * N), bf16),
            pltpu.VMEM((tok, width), bf16),
            pltpu.VMEM((2 * share, gw), bf16),
            pltpu.VMEM((groups, tok, 2 * share), bf16),
            pltpu.VMEM((groups, tok + 16, 2 * share), bf16),
            pltpu.VMEM((groups, 1, 128), f32),
            pltpu.VMEM((groups, tok, N), bf16),
            pltpu.VMEM((groups, tok, N), bf16),
            pltpu.VMEM((CHUNKS, groups, tok, cw), bf16),
            pltpu.VMEM((groups, 1, 128), f32),
            pltpu.VMEM((groups, 1, gw), f32),
            pltpu.VMEM((SLOTS, groups, N, cw), f32),
            pltpu.VMEM((CHUNKS, N, cw), f32),
            pltpu.VMEM((CHUNKS, 1, cw), f32),
            pltpu.VMEM((N, cw), f32),
            pltpu.VMEM((CHUNKS, N, cw), bf16),
            pltpu.VMEM((CHUNKS, 8, cw), f32),
            pltpu.VMEM((CHUNKS, N, cw), bf16),
            pltpu.VMEM((CHUNKS, 8, cw), f32),
            pltpu.VMEM((CHUNKS, N, cw), bf16),
            pltpu.VMEM((CHUNKS, N, cw), bf16),
            pltpu.VMEM((CHUNKS, groups, tok, cw), bf16),
            pltpu.VMEM((tok, width), bf16),
            pltpu.VMEM((tok, width), f32),
            dma((7,)),
            dma,
            dma,
            dma,
            dma((CHUNKS,)),
            dma((CHUNKS,)),
            dma((CHUNKS,)),
            dma((CHUNKS,)),
            dma((CHUNKS, 4)),
            dma,
            dma,
            dma,
            dma((CHUNKS,)),
            dma((CHUNKS, groups)),
            dma((CHUNKS,)),
            dma((CHUNKS,)),
            dma((CHUNKS,)),
        ],
        compiler_params=pltpu.CompilerParams(
            collective_id=0, has_side_effects=True, vmem_limit_bytes=56 * 1024 * 1024
        ),
    )(
        mixer_input,
        step_raw,
        b_proj,
        c_proj,
        step_bias.reshape(1, heads),
        decay_log.reshape(1, heads),
        skip_gain.reshape(1, heads),
    )


def solution(mesh):
    return jax.shard_map(
        body,
        mesh=mesh,
        in_specs=(
            P(("seq", "ctx"), None),
            P(("seq", "ctx"), None),
            P(("seq", "ctx"), None),
            P(("seq", "ctx"), None),
            P(),
            P(),
            P(),
        ),
        out_specs=P(("seq", "ctx"), None),
        check_vma=False,
    )
```

```python
import functools

import jax
import jax.numpy as jnp
from jax import lax
from jax.experimental import pallas as pl
from jax.experimental.pallas import tpu as pltpu
from jax.sharding import PartitionSpec as P

P_SIZE = 64
N = 256
CHUNKS = 8
SLOTS = 4


def scan_kernel(
    nc,
    ns,
    groups,
    x_hbm,
    step_hbm,
    b_hbm,
    c_hbm,
    bias_hbm,
    dlog_hbm,
    gain_hbm,
    o_ref,
    step_ref,
    bias_ref,
    dlog_ref,
    gain_ref,
    xv,
    bv,
    cv,
    xw,
    spread,
    w2,
    ec2,
    dsend,
    rb,
    rc,
    rx,
    rd,
    wide_d,
    states,
    total,
    whole,
    entry,
    pre,
    pre_d,
    run,
    run_d,
    head,
    nexthead,
    offs,
    offr,
    part,
    load_sem,
    sb_sem,
    sc_sem,
    sd_sem,
    sx_sem,
    so_sem,
    sr_sem,
    srd_sem,
    sh_sem,
    rb_sem,
    rc_sem,
    rd_sem,
    rx_sem,
    ro_sem,
    rr_sem,
    rrd_sem,
    rh_sem,
):
    f32, bf16 = jnp.float32, jnp.bfloat16
    me = lax.axis_index("ctx")
    sq = lax.axis_index("seq")
    tok, width = xv.shape
    heads = step_ref.shape[1]
    cw = width // groups // CHUNKS
    share = heads // groups
    gw = share * P_SIZE
    side = groups // 2
    half, span = lax.div(me, groups), lax.rem(me, groups)
    row, col = lax.div(span, side), lax.rem(span, side)
    flip = half * side
    mine = lax.rem(span + flip, groups)
    across = (1 - half) * groups + lax.rem(span + side, groups)
    role = lax.rem(sq, 2) * 2 + half
    block = lax.div(sq, 2)
    blocks = ns // 2
    inner_x = block < blocks - 1

    def partner(k):
        return lax.rem(row + lax.div(k, side), 2) * side + lax.rem(col + lax.rem(k, side), side)

    def source(k):
        return lax.rem(row + lax.div(k, side), 2) * side + lax.rem(
            col + side - lax.rem(k, side), side
        )

    def group_of(s):
        return lax.rem(s + flip, groups)

    def to_ctx(s):
        return {"ctx": half * groups + s}

    def following():
        return {"ctx": across, "seq": jnp.where(role == 1, sq + 1, sq)}

    def preceding():
        return {"ctx": across, "seq": jnp.where(role == 2, sq - 1, sq)}

    def carrier():
        return {
            "ctx": jnp.where(half == 1, me, across),
            "seq": 2 * block - 1,
        }

    def receiver(r):
        return {"ctx": me if r % 2 == 1 else across, "seq": 2 * block + 2 + r // 2}

    barrier = pltpu.get_barrier_semaphore()

    def greet(k, carry):
        pl.semaphore_signal(barrier, inc=1, device_id=to_ctx(partner(k)))
        return carry

    lax.fori_loop(1, groups, greet, 0)

    @pl.when(role > 0)
    def _():
        pl.semaphore_signal(barrier, inc=1, device_id=preceding())

    @pl.when(role < 3)
    def _():
        pl.semaphore_signal(barrier, inc=1, device_id=following())

    @pl.when(block > 0)
    def _():
        pl.semaphore_signal(barrier, inc=1, device_id=carrier())

    @pl.when((role == 3) & inner_x)
    def _():
        for r in range(4):
            pl.semaphore_signal(barrier, inc=1, device_id=receiver(r))

    loads = (
        pltpu.make_async_copy(x_hbm, xv, load_sem.at[0]),
        pltpu.make_async_copy(b_hbm, bv, load_sem.at[1]),
        pltpu.make_async_copy(c_hbm, cv, load_sem.at[2]),
        pltpu.make_async_copy(step_hbm, step_ref, load_sem.at[3]),
        pltpu.make_async_copy(bias_hbm, bias_ref, load_sem.at[4]),
        pltpu.make_async_copy(dlog_hbm, dlog_ref, load_sem.at[5]),
        pltpu.make_async_copy(gain_hbm, gain_ref, load_sem.at[6]),
    )
    for load in loads[3:] + loads[:3]:
        load.start()

    friends = (
        groups
        - 1
        + jnp.where(role > 0, 1, 0)
        + jnp.where(role < 3, 1, 0)
        + jnp.where(block > 0, 1, 0)
        + jnp.where((role == 3) & inner_x, 4, 0)
    )
    pl.semaphore_wait(barrier, friends)

    def columns(start, size):
        return pl.ds(pl.multiple_of(start, 128), size)

    def send_group(src, dst, send_sem, recv_sem):
        def one(k, carry):
            peer = partner(groups - k)
            pltpu.make_async_remote_copy(
                src_ref=src.at[:, columns(group_of(peer) * N, N)],
                dst_ref=dst.at[span],
                send_sem=send_sem,
                recv_sem=recv_sem,
                device_id=to_ctx(peer),
            ).start()
            return carry

        lax.fori_loop(1, groups, one, 0)

    def send_x(c):
        def one(k, carry):
            peer = partner(groups - k)
            pltpu.make_async_remote_copy(
                src_ref=xw.at[:, columns(group_of(peer) * gw + c * cw, cw)],
                dst_ref=rx.at[c, span],
                send_sem=sx_sem.at[c],
                recv_sem=rx_sem.at[c],
                device_id=to_ctx(peer),
            ).start()
            return carry

        lax.fori_loop(1, groups, one, 0)
        pltpu.make_async_copy(
            xw.at[:, columns(mine * gw + c * cw, cw)], rx.at[c, span], rx_sem.at[c]
        ).start()

    send_group(b_hbm, rb, sb_sem, rb_sem)

    for load in loads[3:]:
        load.wait()
    v = step_ref[...].astype(f32) + bias_ref[...]
    dt = jnp.maximum(v, 0.0) + jnp.log1p(jnp.exp(-jnp.abs(v)))
    rate = dt * (-jnp.exp(dlog_ref[...]))
    rows = lax.broadcasted_iota(jnp.int32, (tok, tok), 0)
    cols = lax.broadcasted_iota(jnp.int32, (tok, tok), 1)
    tri = (rows >= cols).astype(f32)
    cum = jnp.dot(tri, rate, precision=lax.Precision.HIGHEST, preferred_element_type=f32)
    w = dt * jnp.exp(-cum)
    ec = jnp.exp(cum)
    w_hi = w.astype(bf16)
    w_lo = (w - w_hi.astype(f32)).astype(bf16)
    e_hi = ec.astype(bf16)
    e_lo = (ec - e_hi.astype(f32)).astype(bf16)
    gain = jnp.broadcast_to(gain_ref[...], (16, heads))
    g_hi = gain.astype(bf16)
    g_lo = (gain - g_hi.astype(f32)).astype(bf16)
    dsend[...] = jnp.zeros(dsend.shape, f32)
    for g in range(groups):
        part_of = slice(g * share, (g + 1) * share)
        w2[g, :, :share] = w_hi[:, part_of]
        w2[g, :, share:] = w_lo[:, part_of]
        ec2[g, :tok, :share] = e_hi[:, part_of]
        ec2[g, :tok, share:] = e_lo[:, part_of]
        ec2[g, tok:, :share] = g_hi[:, part_of]
        ec2[g, tok:, share:] = g_lo[:, part_of]
        dsend[g, :, :share] = ec[tok - 1 :, part_of]
    slot_of = lax.broadcasted_iota(jnp.int32, (2 * share, gw), 0)
    lane_of = lax.broadcasted_iota(jnp.int32, (2 * share, gw), 1)
    spread[...] = jnp.where(lax.rem(slot_of, share) == lax.div(lane_of, P_SIZE), 1.0, 0.0).astype(bf16)

    loads[0].wait()

    def weigh(c):
        def one(g, carry):
            at = columns(g * gw + c * cw, cw)
            weight = jnp.dot(w2[g], spread[:, c * cw : (c + 1) * cw], preferred_element_type=f32)
            xw[:, at] = (xv[:, at].astype(f32) * weight).astype(bf16)
            return carry

        lax.fori_loop(0, groups, one, 0)

    weigh(0)
    send_x(0)

    def send_d(k, carry):
        peer = partner(groups - k)
        pltpu.make_async_remote_copy(
            src_ref=dsend.at[group_of(peer)],
            dst_ref=rd.at[span],
            send_sem=sd_sem,
            recv_sem=rd_sem,
            device_id=to_ctx(peer),
        ).start()
        return carry

    lax.fori_loop(1, groups, send_d, 0)
    pltpu.make_async_copy(dsend.at[mine], rd.at[span], rd_sem).start()
    for c in range(1, CHUNKS):
        weigh(c)
        send_x(c)
        if c == 4:
            send_group(c_hbm, rc, sc_sem, rc_sem)

    loads[1].wait()
    loads[2].wait()
    own = columns(mine * N, N)
    pltpu.make_async_copy(bv.at[:, own], rb.at[span], rb_sem).start()
    pltpu.make_async_copy(cv.at[:, own], rc.at[span], rc_sem).start()

    @pl.when(role == 0)
    def _():
        pre[...] = jnp.zeros(pre.shape, bf16)
        pre_d[...] = jnp.ones(pre_d.shape, f32)

    @pl.when(block == 0)
    def _():
        head[...] = jnp.zeros(head.shape, bf16)

    def local_part(g):
        at = slice(g * gw, (g + 1) * gw)
        state_at = slice(g * N, (g + 1) * N)
        inner = lax.dot_general(
            cv[:, state_at], bv[:, state_at], (((1,), (1,)), ((), ())), preferred_element_type=f32
        )
        inner = jnp.where(rows >= cols, inner, 0.0)
        top = inner.astype(bf16)
        rest = (inner - top.astype(f32)).astype(bf16)

        def one(c, carry):
            at = columns(g * gw + c * cw, cw)
            diag = jnp.dot(top, xw[:, at], preferred_element_type=f32)
            diag += jnp.dot(rest, xw[:, at], preferred_element_type=f32)
            scale = jnp.dot(ec2[g], spread[:, columns(c * cw, cw)], preferred_element_type=f32)
            part[:, at] = scale[:tok] * diag + scale[tok : tok + 1] * xv[:, at].astype(f32)
            return carry

        lax.fori_loop(0, CHUNKS, one, 0)

    def widen_decays():
        left = jnp.concatenate([rd[s] for s in range(groups)], axis=0)[:, :share]
        wide = jnp.zeros((groups, gw), f32)
        for _ in range(3):
            term = left.astype(bf16)
            left = left - term.astype(f32)
            wide = wide + jnp.dot(term, spread[:share], preferred_element_type=f32)
        for s in range(groups):
            wide_d[s] = wide[s : s + 1]

    def decay_row(c, s):
        return wide_d[s, :, c * cw : (c + 1) * cw]

    def gather_states(c):
        pltpu.make_async_copy(rx.at[c], rx.at[c], rx_sem.at[c]).wait()
        slot = c % SLOTS
        total[c] = jnp.zeros(total.shape[1:], f32)

        def one(s, product):
            piece = lax.dot_general(
                rb[s], rx[c, s], (((0,), (0,)), ((), ())), preferred_element_type=f32
            )
            factor = decay_row(c, s)
            states[slot, s] = piece
            total[c] = factor * (total[c] + piece)
            return product * factor

        whole[c] = lax.fori_loop(0, groups, one, jnp.ones((1, cw), f32))

    def pass_run(c):
        return (
            pltpu.make_async_remote_copy(
                src_ref=run.at[c],
                dst_ref=pre.at[c],
                send_sem=sr_sem.at[c],
                recv_sem=rr_sem.at[c],
                device_id=following(),
            ),
            pltpu.make_async_remote_copy(
                src_ref=run_d.at[c],
                dst_ref=pre_d.at[c],
                send_sem=srd_sem.at[c],
                recv_sem=rrd_sem.at[c],
                device_id=following(),
            ),
        )

    def pass_head(c, r):
        return pltpu.make_async_remote_copy(
            src_ref=nexthead.at[c],
            dst_ref=head.at[c],
            send_sem=sh_sem.at[c, r],
            recv_sem=rh_sem.at[c],
            device_id=receiver(r),
        )

    def compose(c):
        @pl.when(role > 0)
        def _():
            pltpu.make_async_copy(pre.at[c], pre.at[c], rr_sem.at[c]).wait()
            pltpu.make_async_copy(pre_d.at[c], pre_d.at[c], rrd_sem.at[c]).wait()

        ahead = whole[c] * pre[c].astype(f32) + total[c]
        span_d = whole[c] * pre_d[c, :1]

        @pl.when(role < 3)
        def _():
            run[c] = ahead.astype(bf16)
            run_d[c] = jnp.broadcast_to(span_d, run_d.shape[1:])
            for copy in pass_run(c):
                copy.start()

        @pl.when((role == 3) & inner_x)
        def _():
            total[c] = ahead
            whole[c] = span_d

    def forward(c):
        @pl.when((role == 3) & inner_x)
        def _():
            @pl.when(block > 0)
            def _():
                pltpu.make_async_copy(head.at[c], head.at[c], rh_sem.at[c]).wait()

            nexthead[c] = (whole[c] * head[c].astype(f32) + total[c]).astype(bf16)
            for r in (3, 2, 1, 0):
                pass_head(c, r).start()

    def read_states(c):
        @pl.when((block > 0) & ((role < 3) | (block == blocks - 1)))
        def _():
            pltpu.make_async_copy(head.at[c], head.at[c], rh_sem.at[c]).wait()

        slot = c % SLOTS
        entry[...] = pre_d[c, :1] * head[c].astype(f32) + pre[c].astype(f32)

        def one(s, carry):
            state = entry[...]
            offs[c, s] = jnp.dot(rc[s], state.astype(bf16), preferred_element_type=f32).astype(bf16)
            entry[...] = decay_row(c, s) * (state + states[slot, s])
            return carry

        lax.fori_loop(0, groups, one, 0)
        at = columns(mine * gw + c * cw, cw)

        def send(k, carry):
            peer = partner(groups - k)
            pltpu.make_async_remote_copy(
                src_ref=offs.at[c, peer],
                dst_ref=offr.at[:, at],
                send_sem=so_sem.at[c],
                recv_sem=ro_sem.at[c, span],
                device_id=to_ctx(peer),
            ).start()
            return carry

        lax.fori_loop(1, groups, send, 0)
        pltpu.make_async_copy(offs.at[c, span], offr.at[:, at], ro_sem.at[c, span]).start()

    def combine(c):
        def one(k, carry):
            s = source(lax.rem(groups - k, groups))
            g = group_of(s)
            at = columns(g * gw + c * cw, cw)
            pltpu.make_async_copy(offs.at[c, 0], offr.at[:, at], ro_sem.at[c, s]).wait()
            scale = jnp.dot(
                ec2[g, :tok, :], spread[:, c * cw : (c + 1) * cw], preferred_element_type=f32
            )
            o_ref[:, at] = (part[:, at] + scale * offr[:, at].astype(f32)).astype(bf16)
            return carry

        lax.fori_loop(0, groups, one, 0)

    pltpu.make_async_copy(rb, rb, rb_sem).wait()
    pltpu.make_async_copy(rd, rd, rd_sem).wait()
    widen_decays()
    lag = SLOTS - 1
    for c in range(CHUNKS + lag):
        if c < CHUNKS:
            gather_states(c)
            compose(c)
            forward(c)
        if c == lag:
            pltpu.make_async_copy(rc, rc, rc_sem).wait()
        if c >= lag:
            read_states(c - lag)
        if c < groups:
            local_part(c)
        if c >= CHUNKS:
            combine(c - CHUNKS)
    for c in range(lag, CHUNKS):
        combine(c)

    for c in range(CHUNKS):
        pltpu.make_async_copy(rx.at[c, 1:], rx.at[c, 1:], sx_sem.at[c]).wait()
        pltpu.make_async_copy(offs.at[c, 1:], offs.at[c, 1:], so_sem.at[c]).wait()

        @pl.when(role < 3)
        def _():
            for copy in pass_run(c):
                copy.wait_send()

        @pl.when((role == 3) & inner_x)
        def _():
            for r in range(4):
                pass_head(c, r).wait_send()

    pltpu.make_async_copy(rb.at[1:], rb.at[1:], sb_sem).wait()
    pltpu.make_async_copy(rc.at[1:], rc.at[1:], sc_sem).wait()
    pltpu.make_async_copy(rd.at[1:], rd.at[1:], sd_sem).wait()


def body(mixer_input, step_raw, b_proj, c_proj, step_bias, decay_log, skip_gain):
    nc, ns = lax.axis_size("ctx"), lax.axis_size("seq")
    tok, width = mixer_input.shape
    heads = step_raw.shape[1]
    groups = b_proj.shape[1] // N
    share = heads // groups
    gw = share * P_SIZE
    cw = gw // CHUNKS
    f32, bf16 = jnp.float32, jnp.bfloat16
    any_spec = pl.BlockSpec(memory_space=pl.ANY)
    vmem_spec = pl.BlockSpec(memory_space=pltpu.VMEM)
    dma = pltpu.SemaphoreType.DMA
    return pl.pallas_call(
        functools.partial(scan_kernel, nc, ns, groups),
        out_shape=pltpu.VMEM((tok, width), bf16),
        in_specs=[any_spec] * 7,
        out_specs=vmem_spec,
        scratch_shapes=[
            pltpu.VMEM((tok, heads), bf16),
            pltpu.VMEM((1, heads), f32),
            pltpu.VMEM((1, heads), f32),
            pltpu.VMEM((1, heads), f32),
            pltpu.VMEM((tok, width), bf16),
            pltpu.VMEM((tok, groups * N), bf16),
            pltpu.VMEM((tok, groups * N), bf16),
            pltpu.VMEM((tok, width), bf16),
            pltpu.VMEM((2 * share, gw), bf16),
            pltpu.VMEM((groups, tok, 2 * share), bf16),
            pltpu.VMEM((groups, tok + 16, 2 * share), bf16),
            pltpu.VMEM((groups, 1, 128), f32),
            pltpu.VMEM((groups, tok, N), bf16),
            pltpu.VMEM((groups, tok, N), bf16),
            pltpu.VMEM((CHUNKS, groups, tok, cw), bf16),
            pltpu.VMEM((groups, 1, 128), f32),
            pltpu.VMEM((groups, 1, gw), f32),
            pltpu.VMEM((SLOTS, groups, N, cw), f32),
            pltpu.VMEM((CHUNKS, N, cw), f32),
            pltpu.VMEM((CHUNKS, 1, cw), f32),
            pltpu.VMEM((N, cw), f32),
            pltpu.VMEM((CHUNKS, N, cw), bf16),
            pltpu.VMEM((CHUNKS, 8, cw), f32),
            pltpu.VMEM((CHUNKS, N, cw), bf16),
            pltpu.VMEM((CHUNKS, 8, cw), f32),
            pltpu.VMEM((CHUNKS, N, cw), bf16),
            pltpu.VMEM((CHUNKS, N, cw), bf16),
            pltpu.VMEM((CHUNKS, groups, tok, cw), bf16),
            pltpu.VMEM((tok, width), bf16),
            pltpu.VMEM((tok, width), f32),
            dma((7,)),
            dma,
            dma,
            dma,
            dma((CHUNKS,)),
            dma((CHUNKS,)),
            dma((CHUNKS,)),
            dma((CHUNKS,)),
            dma((CHUNKS, 4)),
            dma,
            dma,
            dma,
            dma((CHUNKS,)),
            dma((CHUNKS, groups)),
            dma((CHUNKS,)),
            dma((CHUNKS,)),
            dma((CHUNKS,)),
        ],
        compiler_params=pltpu.CompilerParams(
            collective_id=0, has_side_effects=True, vmem_limit_bytes=56 * 1024 * 1024
        ),
    )(
        mixer_input,
        step_raw,
        b_proj,
        c_proj,
        step_bias.reshape(1, heads),
        decay_log.reshape(1, heads),
        skip_gain.reshape(1, heads),
    )


def solution(mesh):
    return jax.shard_map(
        body,
        mesh=mesh,
        in_specs=(
            P(("seq", "ctx"), None),
            P(("seq", "ctx"), None),
            P(("seq", "ctx"), None),
            P(("seq", "ctx"), None),
            P(),
            P(),
            P(),
        ),
        out_specs=P(("seq", "ctx"), None),
        check_vma=False,
    )
```
